128 devices in a mesh: lat: 32 (over x, z, core), lon: 4 (over y).
Axes of the slice: x: 4, y: 4, z: 4, core: 2. Of those that a mesh axis runs over, the one named last changes fastest.
Arguments:
- spectra: bfloat16 [131072, 8448], P(('lat', 'lon')), may hold values from -6 to 6
- pc_basis: bfloat16 [8448, 256], replicated, may hold values from -0.0625 to 0.0625
- destination: int32 [131072, 1], P(('lat', 'lon')), may hold values from 0 to 127; in each aligned block of 1024 rows (0 to 1023, 1024 to 2047, ...) at most 16 rows name the same one
- corner_row: int32 [131072], P(('lat', 'lon')), may hold values from 0 to 64
- corner_col: int32 [131072], P(('lat', 'lon')), may hold values from 0 to 64
- corner_weight: bfloat16 [131072, 4], P(('lat', 'lon')), may hold values from 0 to 1
- state: bfloat16 [2048, 256, 128], P('lat', 'lon'), may hold values from -6 to 6
- inv_sigma: float32 [256], replicated, may hold values from 0.5 to 2
- w_in: bfloat16 [128, 512], replicated, may hold values from -0.5 to 0.5
- b_in: float32 [512], replicated, may hold values from -3 to 3
- w_out: bfloat16 [512, 256], replicated, may hold values from -0.25 to 0.25
- b_out: float32 [256], replicated, may hold values from -3 to 3
Outputs:
- departures: bfloat16 [131072, 256], P(('lat', 'lon'))
- state_gradient: float32 [2048, 256, 128], P('lat', 'lon')
The draws below stay inside these ranges and needn't reach their ends.
Inputs may be any that keep to these rules, and one draw needn't show every extreme that they name: `destination`: in the rows of one device no tile is named by more than 16 spectra, a bound that some block reaches.
All inputs are finite; a program needn't handle non-finite values.
Results may differ from the reference program's by a relative error of at most 0.0075.
Values may be sent and summed in bfloat16 or wider, within the bound.
No kernel may reach another device: no remote copies, remote signals or barrier semaphores. Data moves between devices by JAX's collectives and lax.ppermute only.
A program may use at most 128 MiB of HBM per device.

```python
import math
import jax
import jax.numpy as jnp
import numpy as np
from jax import lax

NCH = 8448
NPC = 256
LEV = 128
HID = 512
OBS_DEV = 1024
ROWS_T = 64
COLS_T = 64
CAP = 16
OBS = 131072
NLAT = 2048
NLON = 256
N_LAT = 32
N_LON = 4


def touch_ends(result, rng, low, largest):
    index_at = [jax.random.randint(jax.random.fold_in(rng, axis), (), 0, length) for axis, length in enumerate(result.shape)]
    widest = result.shape.index(max(result.shape))
    next_to = index_at[:widest] + [(index_at[widest] + 1) % result.shape[widest]] + index_at[widest + 1:]
    return result.at[tuple(index_at)].set(low).at[tuple(next_to)].set(largest)


def level_of(rng, shape, split, smallest, largest):
    loudness = 1.0
    for axis_at, shards_of in split:
        heights = jax.random.uniform(jax.random.fold_in(jax.random.fold_in(rng, 6), axis_at), (shards_of,), jnp.float32, smallest / len(split), largest / len(split))
        loudness = loudness * jnp.repeat(jnp.exp(heights), shape[axis_at] // shards_of).reshape((-1,) + (1,) * (len(shape) - 1 - axis_at))
    return loudness


def routed_block(stream_key, own, number, rows, count, top, reach, lean):
    sequence = jax.random.permutation(stream_key, count)
    packed, ordinary = load_shares(count, rows * top, reach, lean, True), load_shares(count, rows * top, reach, lean, False)
    places = jnp.arange(count)

    def named(sizes, offset_by):
        used = int((sizes > 0).sum())
        fixed = max(1, used // 4)
        passed = fixed + (places - fixed + offset_by * (used - fixed)) % max(1, count - fixed)
        return jnp.zeros((count,), jnp.int32).at[sequence[jnp.where(places < fixed, places, passed)]].set(jnp.asarray(sizes, jnp.int32))

    sizes = jnp.where(number % 4 == 0, named(packed, number // 4), named(ordinary, number - number // 4 - 1))
    mixed = jax.random.permutation(jax.random.fold_in(own, 3), count)
    donor, taker = mixed[0:count // 2 * 2:2], mixed[1:count // 2 * 2:2]
    margin = jnp.minimum(sizes[donor] - 1, reach - sizes[taker]) // 2
    margin = jnp.where((donor == sequence[0]) | (taker == sequence[0]) | (sizes[taker] == 0), 0, jnp.maximum(margin, 0))
    passed = jax.random.randint(jax.random.fold_in(own, 4), (count // 2,), 0, 1 << 20) % (margin + 1)
    sizes = sizes.at[donor].add(-passed).at[taker].add(passed)
    items = jnp.searchsorted(jnp.cumsum(sizes), jnp.arange(rows * top), side="right").astype(jnp.int32)
    table = items.reshape(top, rows).T
    table = table[jax.random.permutation(jax.random.fold_in(own, 1), rows)]
    offset_by = jax.random.randint(jax.random.fold_in(own, 2), (rows, 1), 0, top)
    return jnp.take_along_axis(table, (jnp.arange(top)[None, :] + offset_by) % top, axis=1)


def load_shares(number_of, total, most, skew, full):
    loads = [(1 << 20) // math.isqrt(rank ** skew) + 1 for rank in range(1, number_of + 1)]
    largest = most if full else min(most, max(-(-total // number_of), total * loads[0] // sum(loads)))
    least = 1 if total - largest >= number_of - 1 else 0
    holding, rest = [largest] + [least] * (number_of - 1), total - largest - least * (number_of - 1)
    while rest > 0:
        candidates = [i for i in range(1, number_of) if holding[i] < largest] or [i for i in range(1, number_of) if holding[i] < most]
        pool, remaining = sum([loads[i] for i in candidates]), rest
        for i in candidates:
            more = min(most - holding[i], max(1, remaining * loads[i] // pool), rest)
            holding[i] = holding[i] + more
            rest = rest - more
    return np.array(holding)


def scatter_about(key, shape, width, reach, cuts=(), dtype=jnp.bfloat16):
    result = jax.random.normal(key, shape, jnp.float32) * width
    if len(cuts) > 0:
        result = level_of(key, shape, cuts, -0.22, 0.18) * result
    return jnp.clip(result, min=-reach, max=reach).astype(dtype)


def setup_inputs(seed: int = 0) -> dict:
    key_of = jax.random.split(jax.random.key(seed), 13)
    spectra = scatter_about(key_of[0], (OBS, NCH), 1.0, 6.0, ((0, 128),))
    pc_basis = scatter_about(key_of[1], (NCH, NPC), NCH ** -0.5, 0.0625)
    destination_keys = jax.random.split(jax.random.fold_in(key_of[2], 1), OBS // OBS_DEV)
    destination_turns = jax.random.permutation(jax.random.fold_in(key_of[2], 3), OBS // OBS_DEV)
    destination = jax.vmap(lambda own, number: routed_block(jax.random.fold_in(key_of[2], 2), own, number, OBS_DEV, N_LAT * N_LON, 1, CAP, 2))(destination_keys, destination_turns).reshape((OBS, 1))
    corner_row = touch_ends(jax.random.randint(key_of[3], (OBS,), 0, ROWS_T + 1), jax.random.fold_in(key_of[3], 1), 0, ROWS_T).astype(jnp.int32)
    corner_col = touch_ends(jax.random.randint(key_of[4], (OBS,), 0, COLS_T + 1), jax.random.fold_in(key_of[4], 1), 0, COLS_T).astype(jnp.int32)
    corner_weight = jnp.clip(1.0 * jax.random.uniform(key_of[5], (OBS, 4), jnp.float32) ** level_of(key_of[5], (OBS, 4), ((0, 128),), -0.2, 0.2), 0.0, 1.0).astype(jnp.bfloat16)
    state = scatter_about(key_of[6], (NLAT, NLON, LEV), 1.0, 6.0, ((0, 32), (1, 4)))
    inv_sigma = jnp.clip(jnp.exp(jax.random.uniform(key_of[7], (NPC,), jnp.float32, math.log(0.5), math.log(2.0))), 0.5, 2.0)
    w_in = scatter_about(key_of[8], (LEV, HID), LEV ** -0.5, 0.5)
    b_in = scatter_about(key_of[9], (HID,), 0.5, 3.0, (), jnp.float32)
    w_out = scatter_about(key_of[10], (HID, NPC), HID ** -0.5, 0.25)
    b_out = scatter_about(key_of[11], (NPC,), 0.5, 3.0, (), jnp.float32)
    return {"spectra": spectra, "pc_basis": pc_basis, "destination": destination, "corner_row": corner_row, "corner_col": corner_col, "corner_weight": corner_weight, "state": state, "inv_sigma": inv_sigma, "w_in": w_in, "b_in": b_in, "w_out": w_out, "b_out": b_out}


def reference(spectra, pc_basis, destination, corner_row, corner_col, corner_weight, state, inv_sigma, w_in, b_in, w_out, b_out):
    blocks = spectra.reshape(N_LAT * N_LON, OBS_DEV, NCH)
    pcs = lax.map(lambda block: jnp.dot(block, pc_basis, preferred_element_type=jnp.float32).astype(jnp.bfloat16), blocks)
    pcs = pcs.reshape(-1, NPC)
    dest = destination[:, 0]
    band = dest // N_LON
    quarter = dest % N_LON
    nlon = COLS_T * N_LON
    padded = jnp.pad(state, ((1, 1), (0, 0), (0, 0)))
    rows_base = band * ROWS_T + corner_row
    cols_base = quarter * COLS_T + corner_col - 1
    offsets = [(0, 0), (1, 0), (0, 1), (1, 1)]
    weights = corner_weight.astype(jnp.float32)
    column = jnp.zeros((dest.shape[0], LEV), jnp.float32)
    places = []
    for k in range(4):
        rows_k = (rows_base + offsets[k][0]).astype(jnp.int32)
        cols_k = ((cols_base + offsets[k][1]) % nlon).astype(jnp.int32)
        places.append((rows_k, cols_k))
        column = column + weights[:, k:k + 1] * padded[rows_k, cols_k].astype(jnp.float32)
    column = column.astype(jnp.bfloat16)
    pre = jnp.dot(column, w_in, preferred_element_type=jnp.float32) + b_in
    hidden = jax.nn.silu(pre).astype(jnp.bfloat16)
    sim = jnp.dot(hidden, w_out, preferred_element_type=jnp.float32) + b_out
    dep = (sim - pcs.astype(jnp.float32)) * inv_sigma
    g_sim = (dep * inv_sigma).astype(jnp.bfloat16)
    g_hidden = jnp.dot(g_sim, w_out.T, preferred_element_type=jnp.float32)
    sig = jax.nn.sigmoid(pre)
    g_pre = (g_hidden * sig * (1.0 + pre * (1.0 - sig))).astype(jnp.bfloat16)
    g_column = jnp.dot(g_pre, w_in.T, preferred_element_type=jnp.float32)
    grad = jnp.zeros(padded.shape, jnp.float32)
    for k in range(4):
        grad = grad.at[places[k][0], places[k][1]].add(weights[:, k:k + 1] * g_column)
    return dep.astype(jnp.bfloat16), grad[1:-1]
```

```python
import jax
import jax.numpy as jnp
from jax import lax
from jax.experimental import pallas as pl
from jax.experimental.pallas import tpu as pltpu
from jax.sharding import PartitionSpec as P

CAP = 16
F32 = jnp.float32
BF16 = jnp.bfloat16
I32 = jnp.int32
NT = (((1,), (1,)), ((), ()))
AXES = ("lat", "lon")


def iota(shape, dim):
    return lax.broadcasted_iota(I32, shape, dim)


def mm(a, b):
    return jnp.dot(a, b, preferred_element_type=F32)


def ones_where(mask):
    return jnp.where(mask, 1.0, 0.0).astype(BF16)


def call(body, out_shape, name, *args, scratch=()):
    return pl.pallas_call(body, out_shape=out_shape, scratch_shapes=scratch, name=name)(*args)


def route_body(dest_ref, row_ref, col_ref, weight_ref, state_ref, send_ref, place_ref, first_ref, last_ref):
    first_ref[...] = state_ref[:, 0, :]
    last_ref[...] = state_ref[:, 63, :]
    dest = dest_ref[...]
    tiles = send_ref.shape[0]
    obs = dest.shape[1]
    onehot = jnp.where(iota((tiles, obs), 0) == dest, 1.0, 0.0)
    before = ones_where(iota((obs, obs), 0) < iota((obs, obs), 1))
    rank = mm(onehot.astype(BF16), before)
    slot = jnp.sum(onehot * rank, axis=0, keepdims=True).astype(I32)
    place_ref[...] = dest * CAP + slot
    here = iota((CAP, obs), 0) == slot
    weights = weight_ref[...].astype(F32)
    fields = [weights[k : k + 1] for k in range(4)]
    fields += [row_ref[...].astype(F32), col_ref[...].astype(F32)]
    parts = [jnp.where(here, field, 0.0) for field in fields]
    parts.append(jnp.zeros((128 - CAP * len(parts), obs), F32))
    table = jnp.concatenate(parts, 0).astype(BF16)
    send_ref[...] = lax.dot_general(onehot.astype(BF16), table, NT, preferred_element_type=F32)


def fields_by_row(recv, first, count):
    tiles = recv.shape[0]
    pick = ones_where((iota((count, tiles), 0) + first) // CAP == iota((count, tiles), 1))
    mine = mm(pick, recv)
    mine = jnp.where(iota((count, 128), 0) % CAP == iota((count, 128), 1) % CAP, mine, 0.0)
    spread = ones_where(iota((128, 768), 0) // CAP == iota((128, 768), 1) // 128)
    out = mm(mine.astype(BF16), spread)
    return [out[:, 128 * k : 128 * k + 128] for k in range(6)]


def fields_by_lane(recv, slots):
    tiles = recv.shape[0]
    pick = ones_where(iota((tiles, slots), 1) // CAP == iota((tiles, slots), 0))
    mine = mm(recv.astype(F32).T.astype(BF16), pick)
    mine = jnp.where(iota((128, slots), 1) % CAP == iota((128, slots), 0) % CAP, mine, 0.0)
    gather = ones_where(iota((8, 128), 1) // CAP == iota((8, 128), 0))
    out = mm(gather, mine.astype(BF16))
    return [out[k : k + 1] for k in range(6)]


def pair_of(hit0, value0, hit1, value1):
    return jnp.where(hit0, value0, jnp.where(hit1, value1, jnp.zeros((), value0.dtype)))


def gather_body(recv_ref, own_ref, top_ref, bottom_ref, left_ref, right_ref, out_ref, matrix_ref, rim_ref):
    slots = out_ref.shape[0]
    chunk = matrix_ref.shape[0]
    rim_ref[0:64, :] = top_ref[0:64, :]
    rim_ref[64:128, :] = bottom_ref[0:64, :]
    rim_ref[128:192, :] = left_ref[...]
    rim_ref[192:256, :] = right_ref[...]
    rim_ref[256:272, :] = top_ref[64:80, :]
    rim_ref[272:288, :] = bottom_ref[64:80, :]
    rim_ref[288:384, :] = jnp.zeros((96, rim_ref.shape[1]), BF16)
    recv = recv_ref[...].astype(BF16)
    shape = (chunk, 128)
    lane = iota(shape, 1).astype(F32)
    high = lane >= 64.0
    upper = jnp.where(high, 1.0, 0.0)
    in_row = lane - 64.0 * upper

    def step(i, carry):
        first = i * chunk
        w0, w1, w2, w3, row, col = fields_by_row(recv, first, chunk)
        at0, at1 = in_row == col - 1.0, in_row == col
        p0 = pair_of(at0, w0, at1, w2)
        p1 = pair_of(at0, w1, at1, w3)
        edge = 65.0 * upper
        matrix_ref[:, 4096:4224] = pair_of(edge == row, p0, edge == row + 1.0, p1).astype(BF16)
        side = pair_of(in_row == row - 1.0, jnp.where(high, w2, w0), in_row == row, jnp.where(high, w3, w1))
        matrix_ref[:, 4224:4352] = jnp.where(col == 64.0 * upper, side, 0.0).astype(BF16)
        corner = pair_of(lane == 0.0, w0, lane == 16.0, w1) + pair_of(lane == 1.0, w2, lane == 17.0, w3)
        at_row = jnp.where(lane < 16.0, 0.0, 64.0)
        at_col = jnp.where((lane == 1.0) | (lane == 17.0), 64.0, 0.0)
        matrix_ref[:, 4352:4480] = jnp.where((row == at_row) & (col == at_col), corner, 0.0).astype(BF16)
        p0, p1, offset = p0.astype(BF16), p1.astype(BF16), (row - upper).astype(BF16)
        for j in range(32):
            matrix_ref[:, 128 * j : 128 * j + 128] = pair_of(offset == 2.0 * j + 1.0, p0, offset == 2.0 * j, p1)
        out = mm(matrix_ref[:, :4096], own_ref[...]) + mm(matrix_ref[:, 4096:], rim_ref[...])
        out_ref[pl.ds(pl.multiple_of(first, chunk), chunk), :] = out.astype(BF16)
        return carry

    lax.fori_loop(0, slots // chunk, step, 0)


def components_body(spectra_ref, basis_ref, place_ref, send_ref, pcs_ref, pick_ref):
    i = pl.program_id(0)
    rows = spectra_ref.shape[0]
    slots = send_ref.shape[0]
    at = pl.ds(pl.multiple_of(i * rows, rows), rows)
    pcs_ref[at, :] = mm(spectra_ref[...], basis_ref[...]).astype(BF16)
    pick_ref[:, at] = ones_where(iota((slots, rows), 0) == place_ref[...])

    @pl.when(i == pl.num_programs(0) - 1)
    def _():
        send_ref[...] = mm(pick_ref[...], pcs_ref[...]).astype(BF16)


def network_body(column_ref, pcs_ref, inv_ref, w_in_ref, b_in_ref, w_out_ref, b_out_ref, dep_ref, g_ref):
    pre = mm(column_ref[...], w_in_ref[...]) + b_in_ref[...]
    sig = jax.nn.sigmoid(pre)
    hidden = (pre * sig).astype(BF16)
    sim = mm(hidden, w_out_ref[...]) + b_out_ref[...]
    inv = inv_ref[...]
    dep = (sim - pcs_ref[...].astype(F32)) * inv
    dep_ref[...] = dep.astype(BF16)
    g_sim = (dep * inv).astype(BF16)
    g_hidden = lax.dot_general(g_sim, w_out_ref[...], NT, preferred_element_type=F32)
    g_pre = (g_hidden * sig * (1.0 + pre * (1.0 - sig))).astype(BF16)
    g_ref[...] = lax.dot_general(g_pre, w_in_ref[...], NT, preferred_element_type=F32).astype(BF16)


def unpack_body(back_ref, place_ref, out_ref, pick_ref):
    slots = back_ref.shape[0]
    obs = out_ref.shape[0]
    rows = jnp.broadcast_to(place_ref[...].astype(F32), (128, obs)).T
    lane = iota((obs, 128), 1).astype(F32)
    for b in range(slots // 128):
        pick_ref[:, 128 * b : 128 * b + 128] = ones_where(rows - 128.0 * b == lane)
    out_ref[...] = mm(pick_ref[...], back_ref[...]).astype(BF16)


def scatter_rim_body(recv_ref, g_ref, up_ref, down_ref, left_ref, right_ref, matrix_ref):
    slots = g_ref.shape[0]
    w0, w1, w2, w3, row, col = fields_by_lane(recv_ref[...].astype(BF16), slots)
    sub = iota((64, slots), 0).astype(F32)
    at0, at1 = sub == col - 1.0, sub == col
    matrix_ref[0:64, :] = jnp.where(row == 0.0, pair_of(at0, w0, at1, w2), 0.0).astype(BF16)
    matrix_ref[80:144, :] = jnp.where(row == 64.0, pair_of(at0, w1, at1, w3), 0.0).astype(BF16)
    at0, at1 = sub == row - 1.0, sub == row
    matrix_ref[160:224, :] = jnp.where(col == 0.0, pair_of(at0, w0, at1, w1), 0.0).astype(BF16)
    matrix_ref[224:288, :] = jnp.where(col == 64.0, pair_of(at0, w2, at1, w3), 0.0).astype(BF16)
    sub = iota((16, slots), 0).astype(F32)
    at0, at1 = (sub == 0.0) & (col == 0.0), (sub == 1.0) & (col == 64.0)
    matrix_ref[64:80, :] = jnp.where(row == 0.0, pair_of(at0, w0, at1, w2), 0.0).astype(BF16)
    matrix_ref[144:160, :] = jnp.where(row == 64.0, pair_of(at0, w1, at1, w3), 0.0).astype(BF16)
    out = mm(matrix_ref[...], g_ref[...])
    up_ref[...] = out[0:80].astype(BF16)
    down_ref[...] = out[80:160].astype(BF16)
    left_ref[...] = out[160:224]
    right_ref[...] = out[224:288]


def scatter_body(recv_ref, g_ref, out_ref, matrix_ref):
    slots = g_ref.shape[0]
    rows = matrix_ref.shape[0] // 64
    w0, w1, w2, w3, row, col = fields_by_lane(recv_ref[...].astype(BF16), slots)
    sub = iota((64, slots), 0).astype(F32)
    at0, at1 = sub == col - 1.0, sub == col
    p0 = pair_of(at0, w0, at1, w2).astype(BF16)
    p1 = pair_of(at0, w1, at1, w3).astype(BF16)
    row = jnp.broadcast_to(row, (64, slots)).astype(BF16)

    def step(i, carry):
        base = (i * rows).astype(F32)
        for j in range(rows):
            at = base + j
            matrix_ref[64 * j : 64 * j + 64, :] = pair_of(row == (at + 1.0).astype(BF16), p0, row == at.astype(BF16), p1)
        out = mm(matrix_ref[...], g_ref[...])
        out_ref[pl.ds(i * rows, rows)] = out.reshape(rows, 64, out.shape[1])
        return carry

    lax.fori_loop(0, 64 // rows, step, 0)


def shift(x, axis, step, closed):
    count = lax.axis_size(axis)
    pairs = [(i, (i + step) % count) for i in range(count) if closed or 0 <= i + step < count]
    return lax.ppermute(x, axis, pairs)


def exchange(x):
    return lax.all_to_all(x, AXES, split_axis=0, concat_axis=0, tiled=True)


def per_device(
    spectra,
    pc_basis,
    destination,
    corner_row,
    corner_col,
    corner_weight,
    state,
    inv_sigma,
    w_in,
    b_in,
    w_out,
    b_out,
):
    tiles = lax.axis_size("lat") * lax.axis_size("lon")
    obs = spectra.shape[0]
    npc = pc_basis.shape[1]
    levels = state.shape[2]
    slots = tiles * CAP
    sds = jax.ShapeDtypeStruct

    send_meta, place, first, last = call(
        route_body,
        (sds((tiles, 128), F32), sds((1, obs), I32), sds((64, levels), BF16), sds((64, levels), BF16)),
        "route",
        destination.reshape(1, obs),
        corner_row.reshape(1, obs),
        corner_col.reshape(1, obs),
        corner_weight.T,
        state,
    )
    recv_meta = exchange(send_meta)

    left = shift(last, "lon", 1, True)
    right = shift(first, "lon", -1, True)
    fill = jnp.zeros((14, levels), BF16)
    top = shift(jnp.concatenate([state[63], left[63:], right[63:], fill], 0), "lat", 1, False)
    bottom = shift(jnp.concatenate([state[0], left[:1], right[:1], fill], 0), "lat", -1, False)

    rows = obs // 4
    send_pcs = pl.pallas_call(
        components_body,
        grid=(obs // rows,),
        in_specs=[
            pl.BlockSpec((rows, spectra.shape[1]), lambda i: (i, 0)),
            pl.BlockSpec(pc_basis.shape, lambda i: (0, 0)),
            pl.BlockSpec((1, rows), lambda i: (0, i)),
        ],
        out_specs=pl.BlockSpec((slots, npc), lambda i: (0, 0)),
        out_shape=sds((slots, npc), BF16),
        scratch_shapes=[pltpu.VMEM((obs, npc), BF16), pltpu.VMEM((slots, obs), BF16)],
        name="components",
    )(spectra, pc_basis, place)
    recv_pcs = exchange(send_pcs.reshape(tiles, CAP, npc)).reshape(slots, npc)

    columns = call(
        gather_body,
        sds((slots, levels), BF16),
        "interpolate",
        recv_meta,
        state.reshape(-1, levels),
        top,
        bottom,
        left,
        right,
        scratch=[pltpu.VMEM((512, 4480), BF16), pltpu.VMEM((384, levels), BF16)],
    )

    def whole(x):
        return pl.BlockSpec(x.shape, lambda i: (0,) * x.ndim)

    block = slots // 4
    constants = (inv_sigma[None], w_in, b_in[None], w_out, b_out[None])
    dep, g = pl.pallas_call(
        network_body,
        grid=(slots // block,),
        in_specs=[
            pl.BlockSpec((block, levels), lambda i: (i, 0)),
            pl.BlockSpec((block, npc), lambda i: (i, 0)),
            *map(whole, constants),
        ],
        out_specs=[
            pl.BlockSpec((block, npc), lambda i: (i, 0)),
            pl.BlockSpec((block, levels), lambda i: (i, 0)),
        ],
        out_shape=(sds((slots, npc), BF16), sds((slots, levels), BF16)),
        name="network",
    )(columns, recv_pcs, *constants)
    back = exchange(dep.reshape(tiles, CAP, npc)).reshape(slots, npc)

    up, down, g_left, g_right = call(
        scatter_rim_body,
        (sds((80, levels), BF16), sds((80, levels), BF16), sds((64, levels), F32), sds((64, levels), F32)),
        "adjoint_rim",
        recv_meta,
        g,
        scratch=[pltpu.VMEM((288, slots), BF16)],
    )
    from_below = shift(up, "lat", -1, False)
    from_above = shift(down, "lat", 1, False)
    gradient = call(
        scatter_body,
        sds((64, 64, levels), F32),
        "adjoint",
        recv_meta,
        g,
        scratch=[pltpu.VMEM((512, slots), BF16)],
    )
    above, below = from_above[64:66].astype(F32), from_below[64:66].astype(F32)
    g_left = g_left.at[0].add(above[0]).at[63].add(below[0])
    g_right = g_right.at[0].add(above[1]).at[63].add(below[1])
    from_right = shift(g_left.astype(BF16), "lon", -1, True)
    from_left = shift(g_right.astype(BF16), "lon", 1, True)
    gradient = call(
        edge_body,
        sds((64, 64, levels), F32),
        "edges",
        gradient,
        from_left,
        from_right,
        from_above,
        from_below,
    )
    departures = call(
        unpack_body,
        sds((obs, npc), BF16),
        "unpack",
        back,
        place,
        scratch=[pltpu.VMEM((obs, slots), BF16)],
    )
    return (departures, gradient)


def edge_body(grad_ref, left_ref, right_ref, above_ref, below_ref, out_ref):
    out_ref[...] = grad_ref[...]
    out_ref[0] += above_ref[0:64, :].astype(F32)
    out_ref[63] += below_ref[0:64, :].astype(F32)
    out_ref[:, 0, :] += left_ref[...].astype(F32)
    out_ref[:, 63, :] += right_ref[...].astype(F32)


def solution(mesh):
    return jax.shard_map(
        per_device,
        mesh=mesh,
        in_specs=(
            P(AXES, None),
            P(),
            P(AXES, None),
            P(AXES),
            P(AXES),
            P(AXES, None),
            P("lat", "lon", None),
            P(),
            P(),
            P(),
            P(),
            P(),
        ),
        out_specs=(P(AXES, None), P("lat", "lon", None)),
        check_vma=False,
    )
```

```python
import jax
import jax.numpy as jnp
from jax import lax
from jax.experimental import pallas as pl
from jax.experimental.pallas import tpu as pltpu
from jax.sharding import PartitionSpec as P

CAP = 16
F32 = jnp.float32
BF16 = jnp.bfloat16
I32 = jnp.int32
NT = (((1,), (1,)), ((), ()))
AXES = ("lat", "lon")


def iota(shape, dim):
    return lax.broadcasted_iota(I32, shape, dim)


def mm(a, b):
    return jnp.dot(a, b, preferred_element_type=F32)


def ones_where(mask):
    return jnp.where(mask, 1.0, 0.0).astype(BF16)


def call(body, out_shape, name, *args, scratch=(), specs=None, outs=None, grant=8, alias=None):
    vmem = pl.BlockSpec(memory_space=pltpu.VMEM)
    return pl.pallas_call(
        body,
        in_specs=specs or [vmem] * len(args),
        out_specs=outs or jax.tree.map(lambda s: vmem, out_shape),
        out_shape=out_shape,
        scratch_shapes=scratch,
        input_output_aliases=alias or {},
        compiler_params=pltpu.CompilerParams(vmem_limit_bytes=grant << 20) if grant else None,
        name=name,
    )(*args)


def route_body(dest_ref, row_ref, col_ref, weight_ref, state_ref, send_ref, place_ref, first_ref, last_ref):
    first_ref[...] = state_ref[:, 0, :]
    last_ref[...] = state_ref[:, 63, :]
    dest = dest_ref[...]
    tiles = send_ref.shape[0]
    obs = dest.shape[1]
    onehot = jnp.where(iota((tiles, obs), 0) == dest, 1.0, 0.0)
    before = ones_where(iota((obs, obs), 0) < iota((obs, obs), 1))
    rank = mm(onehot.astype(BF16), before)
    slot = jnp.sum(onehot * rank, axis=0, keepdims=True).astype(I32)
    place_ref[...] = dest * CAP + slot
    here = iota((CAP, obs), 0) == slot
    weights = weight_ref[...].astype(F32)
    fields = [weights[k : k + 1] for k in range(4)]
    fields += [row_ref[...].astype(F32), col_ref[...].astype(F32)]
    parts = [jnp.where(here, field, 0.0) for field in fields]
    parts.append(jnp.zeros((128 - CAP * len(parts), obs), F32))
    table = jnp.concatenate(parts, 0).astype(BF16)
    send_ref[...] = lax.dot_general(onehot.astype(BF16), table, NT, preferred_element_type=F32)


def fields_by_row(recv, first, count):
    tiles = recv.shape[0]
    pick = ones_where((iota((count, tiles), 0) + first) // CAP == iota((count, tiles), 1))
    mine = mm(pick, recv)
    mine = jnp.where(iota((count, 128), 0) % CAP == iota((count, 128), 1) % CAP, mine, 0.0)
    spread = ones_where(iota((128, 768), 0) // CAP == iota((128, 768), 1) // 128)
    out = mm(mine.astype(BF16), spread)
    return [out[:, 128 * k : 128 * k + 128] for k in range(6)]


def fields_by_lane(recv, slots):
    tiles = recv.shape[0]
    pick = ones_where(iota((tiles, slots), 1) // CAP == iota((tiles, slots), 0))
    mine = mm(recv.astype(F32).T.astype(BF16), pick)
    mine = jnp.where(iota((128, slots), 1) % CAP == iota((128, slots), 0) % CAP, mine, 0.0)
    gather = ones_where(iota((8, 128), 1) // CAP == iota((8, 128), 0))
    out = mm(gather, mine.astype(BF16))
    return [out[k : k + 1] for k in range(6)]


def pair_of(hit0, value0, hit1, value1):
    return jnp.where(hit0, value0, jnp.where(hit1, value1, jnp.zeros((), value0.dtype)))


def gather_body(recv_ref, own_ref, top_ref, bottom_ref, left_ref, right_ref, out_ref, rim_ref, *matrices):
    slots = out_ref.shape[0]
    chunk = matrices[0].shape[0]
    rim_ref[0:64, :] = top_ref[...]
    rim_ref[64:128, :] = bottom_ref[...]
    rim_ref[128:192, :] = left_ref[0:64, :]
    rim_ref[192:256, :] = right_ref[0:64, :]
    rim_ref[256:272, :] = left_ref[64:80, :]
    rim_ref[272:288, :] = right_ref[64:80, :]
    rim_ref[288:384, :] = jnp.zeros((96, rim_ref.shape[1]), BF16)
    recv = recv_ref[...].astype(BF16)
    lane = iota((chunk, 128), 1).astype(F32)
    upper = jnp.where(lane >= 64.0, 1.0, 0.0)
    in_row = (lane - 64.0 * upper).astype(BF16)
    upper = upper.astype(BF16)
    lane = lane.astype(BF16)

    def build(first, matrix_ref):
        w0, w1, w2, w3, row, col = [f.astype(BF16) for f in fields_by_row(recv, first, chunk)]
        at0, at1 = in_row == col - 1.0, in_row == col
        p0 = pair_of(at0, w0, at1, w2)
        p1 = pair_of(at0, w1, at1, w3)
        zero = jnp.zeros((), BF16)
        edge = 65.0 * upper
        matrix_ref[:, 4096:4224] = pair_of(edge == row, p0, edge == row + 1.0, p1)
        high = upper > 0.5
        side = pair_of(in_row == row - 1.0, jnp.where(high, w2, w0), in_row == row, jnp.where(high, w3, w1))
        matrix_ref[:, 4224:4352] = jnp.where(col == 64.0 * upper, side, zero)
        corner = pair_of(lane == 0.0, w0, lane == 1.0, w1) + pair_of(lane == 16.0, w2, lane == 17.0, w3)
        at_col = jnp.where(lane < 16.0, zero, zero + 64.0)
        odd = jnp.where(lane < 16.0, lane, lane - 16.0)
        matrix_ref[:, 4352:4480] = jnp.where(row == 64.0 * odd, jnp.where(col == at_col, corner, zero), zero)
        offset = row - upper
        for j in range(32):
            matrix_ref[:, 128 * j : 128 * j + 128] = pair_of(offset == 2.0 * j + 1.0, p0, offset == 2.0 * j, p1)

    def use(first, matrix_ref):
        out = mm(matrix_ref[:, :4096], own_ref[...]) + mm(matrix_ref[:, 4096:], rim_ref[...])
        out_ref[first : first + chunk, :] = out.astype(BF16)

    count = slots // chunk
    build(0, matrices[0])
    for i in range(count):
        if i + 1 < count:
            build((i + 1) * chunk, matrices[i + 1])
        use(i * chunk, matrices[i])


def components_body(spectra_ref, basis_ref, place_ref, send_ref, back_ref, buffer, pcs_ref, pick_ref, back_buffer, part_ref, out_buffer, sems, back_sem, out_sems, basis_buffer, basis_sem):
    obs = spectra_ref.shape[0]
    slots = send_ref.shape[0]
    blocks = buffer.shape[0]
    rows = obs // blocks
    copies = [
        pltpu.make_async_copy(spectra_ref.at[pl.ds(i * rows, rows), :], buffer.at[i], sems.at[i]) for i in range(blocks)
    ]
    basis = pltpu.make_async_copy(basis_ref, basis_buffer, basis_sem)
    basis.start()
    for copy in copies:
        copy.start()
    place = place_ref[...]
    wide = jnp.broadcast_to(place.astype(F32), (128, obs)).T
    lane = iota((obs, 128), 1).astype(F32)
    for b in range(slots // 128):
        back_buffer[:, 128 * b : 128 * b + 128] = ones_where(wide - 128.0 * b == lane)
    save = pltpu.make_async_copy(back_buffer, back_ref, back_sem)
    save.start()
    for b in range(slots // 256):
        pick_ref[256 * b : 256 * b + 256, :] = ones_where(iota((256, obs), 0) + 256 * b == place)
    for i, copy in enumerate(copies):
        if i == blocks - 1:
            part_ref[...] = mm(pick_ref[:, : i * rows], pcs_ref[: i * rows, :])
        if i == 0:
            basis.wait()
        copy.wait()
        pcs_ref[i * rows : i * rows + rows, :] = mm(buffer[i], basis_buffer[...]).astype(BF16)
    last = obs - rows
    outs = []
    for i in range(4):
        at = slice(i * slots // 4, (i + 1) * slots // 4)
        out_buffer[at, :] = (part_ref[at, :] + mm(pick_ref[at, last:], pcs_ref[last:, :])).astype(BF16)
        outs.append(pltpu.make_async_copy(out_buffer.at[at, :], send_ref.at[at, :], out_sems.at[i]))
        outs[i].start()
    for copy in outs:
        copy.wait()
    save.wait()


def network_body(column_ref, pcs_ref, inv_ref, w_in_ref, b_in_ref, w_out_ref, b_out_ref, dep_ref, g_ref, buffer, sems):
    slots = column_ref.shape[0]
    block = slots // 4
    inv = inv_ref[...]
    copies = []
    for i in range(4):
        at = slice(i * block, (i + 1) * block)
        pre = mm(column_ref[at, :], w_in_ref[...]) + b_in_ref[...]
        sig = jax.nn.sigmoid(pre)
        hidden = (pre * sig).astype(BF16)
        sim = mm(hidden, w_out_ref[...]) + b_out_ref[...]
        dep = (sim - pcs_ref[at, :].astype(F32)) * inv
        buffer[at, :] = dep.astype(BF16)
        copies.append(pltpu.make_async_copy(buffer.at[at, :], dep_ref.at[at, :], sems.at[i]))
        copies[i].start()
        g_sim = (dep * inv).astype(BF16)
        g_hidden = lax.dot_general(g_sim, w_out_ref[...], NT, preferred_element_type=F32)
        g_pre = (g_hidden * sig * (1.0 + pre * (1.0 - sig))).astype(BF16)
        g_ref[at, :] = lax.dot_general(g_pre, w_in_ref[...], NT, preferred_element_type=F32).astype(BF16)
    for copy in copies:
        copy.wait()


def finish_body(back_ref, pick_ref, left_ref, right_ref, above_ref, below_ref, grad_ref, dep_ref, out_ref, picks, sides, rows, sems, in_sems, out_sems):
    edges = [
        (out_ref.at[:, pl.ds(0, 8), :], sides.at[0]),
        (out_ref.at[:, pl.ds(56, 8), :], sides.at[1]),
        (out_ref.at[0, pl.ds(8, 48), :], rows.at[0]),
        (out_ref.at[63, pl.ds(8, 48), :], rows.at[1]),
    ]
    loads = [pltpu.make_async_copy(a, b, in_sems.at[i]) for i, (a, b) in enumerate(edges)]
    stores = [pltpu.make_async_copy(b, a, out_sems.at[i]) for i, (a, b) in enumerate(edges)]
    for copy in loads:
        copy.start()
    obs = dep_ref.shape[0]
    block = obs // 4
    copies = [pltpu.make_async_copy(pick_ref.at[pl.ds(i * block, block), :], picks.at[i], sems.at[i]) for i in range(4)]
    for copy in copies:
        copy.start()
    for copy in loads:
        copy.wait()
    above, below = above_ref[...].astype(F32), below_ref[...].astype(F32)
    sides[0, :, 0, :] += left_ref[0:64, :].astype(F32)
    sides[1, :, 7, :] += right_ref[0:64, :].astype(F32)
    sides[0, 0] += above[0:8]
    sides[1, 0] += above[56:64]
    sides[0, 63] += below[0:8]
    sides[1, 63] += below[56:64]
    rows[0] += above[8:56]
    rows[1] += below[8:56]
    for copy in stores:
        copy.start()
    for i, copy in enumerate(copies):
        copy.wait()
        dep_ref[i * block : i * block + block, :] = mm(picks[i], back_ref[...]).astype(BF16)
    for copy in stores:
        copy.wait()


def scatter_rim_body(recv_ref, g_ref, up_ref, down_ref, left_ref, right_ref, matrix_ref):
    slots = g_ref.shape[0]
    w0, w1, w2, w3, row, col = fields_by_lane(recv_ref[...].astype(BF16), slots)
    sub = iota((64, slots), 0).astype(F32)
    at0, at1 = sub == col - 1.0, sub == col
    matrix_ref[0:64, :] = jnp.where(row == 0.0, pair_of(at0, w0, at1, w2), 0.0).astype(BF16)
    matrix_ref[64:128, :] = jnp.where(row == 64.0, pair_of(at0, w1, at1, w3), 0.0).astype(BF16)
    at0, at1 = sub == row - 1.0, sub == row
    matrix_ref[128:192, :] = jnp.where(col == 0.0, pair_of(at0, w0, at1, w1), 0.0).astype(BF16)
    matrix_ref[208:272, :] = jnp.where(col == 64.0, pair_of(at0, w2, at1, w3), 0.0).astype(BF16)
    sub = iota((16, slots), 0).astype(F32)
    at0, at1 = (sub == 0.0) & (row == 0.0), (sub == 1.0) & (row == 64.0)
    matrix_ref[192:208, :] = jnp.where(col == 0.0, pair_of(at0, w0, at1, w1), 0.0).astype(BF16)
    matrix_ref[272:288, :] = jnp.where(col == 64.0, pair_of(at0, w2, at1, w3), 0.0).astype(BF16)
    out = mm(matrix_ref[...], g_ref[...])
    up_ref[...] = out[0:64]
    down_ref[...] = out[64:128]
    left_ref[...] = out[128:208].astype(BF16)
    right_ref[...] = out[208:288].astype(BF16)


def corner_body(up_ref, down_ref, left_ref, right_ref, up_out, down_out):
    at = iota((64, 128), 0)
    left = left_ref[64:80, :].astype(F32)
    right = right_ref[64:80, :].astype(F32)
    for k, (ref, out) in enumerate(((up_ref, up_out), (down_ref, down_out))):
        extra = jnp.where(at == 0, left[k : k + 1], jnp.where(at == 63, right[k : k + 1], 0.0))
        out[...] = (ref[...] + extra).astype(BF16)


def scatter_body(recv_ref, g_ref, out_ref, buffer, sems, *matrices):
    slots = g_ref.shape[0]
    rows = matrices[0].shape[0] // 64
    w0, w1, w2, w3, row, col = [f.astype(BF16) for f in fields_by_lane(recv_ref[...].astype(BF16), slots)]
    sub = iota((64, slots), 0).astype(F32).astype(BF16)
    at0, at1 = sub == col - 1.0, sub == col
    p0 = pair_of(at0, w0, at1, w2)
    p1 = pair_of(at0, w1, at1, w3)
    row = jnp.broadcast_to(row, (64, slots))

    def build(base, matrix_ref):
        for j in range(rows):
            at = float(base + j)
            matrix_ref[64 * j : 64 * j + 64, :] = pair_of(row == at + 1.0, p0, row == at, p1)

    count = 64 // rows
    copies = []
    build(0, matrices[0])
    for i in range(count):
        if i + 1 < count:
            build((i + 1) * rows, matrices[i + 1])
        out = mm(matrices[i][...], g_ref[...])
        buffer[i * rows : i * rows + rows] = out.reshape(rows, 64, out.shape[1])
        at = pl.ds(i * rows, rows)
        copies.append(pltpu.make_async_copy(buffer.at[at], out_ref.at[at], sems.at[i]))
        copies[i].start()
    for copy in copies:
        copy.wait()


def in_hbm(x):
    return pltpu.with_memory_space_constraint(x, pltpu.HBM)


def shift(x, axis, step, closed):
    count = lax.axis_size(axis)
    pairs = [(i, (i + step) % count) for i in range(count) if closed or 0 <= i + step < count]
    return lax.ppermute(x, axis, pairs)


def exchange(x):
    return lax.all_to_all(x, AXES, split_axis=0, concat_axis=0, tiled=True)


def per_device(
    spectra,
    pc_basis,
    destination,
    corner_row,
    corner_col,
    corner_weight,
    state,
    inv_sigma,
    w_in,
    b_in,
    w_out,
    b_out,
):
    tiles = lax.axis_size("lat") * lax.axis_size("lon")
    obs = spectra.shape[0]
    npc = pc_basis.shape[1]
    levels = state.shape[2]
    slots = tiles * CAP
    sds = jax.ShapeDtypeStruct

    top = shift(state[63], "lat", 1, False)
    bottom = shift(state[0], "lat", -1, False)
    send_meta, place, first, last = call(
        route_body,
        (sds((tiles, 128), F32), sds((1, obs), I32), sds((64, levels), BF16), sds((64, levels), BF16)),
        "route",
        destination.reshape(1, obs),
        corner_row.reshape(1, obs),
        corner_col.reshape(1, obs),
        corner_weight.T,
        state,
        grant=None,
    )
    recv_meta = exchange(send_meta)

    fill = jnp.zeros((14, levels), BF16)
    left = shift(jnp.concatenate([last, top[63:], bottom[63:], fill], 0), "lon", 1, True)
    right = shift(jnp.concatenate([first, top[:1], bottom[:1], fill], 0), "lon", -1, True)

    vmem = pl.BlockSpec(memory_space=pltpu.VMEM)
    hbm = pl.BlockSpec(memory_space=pltpu.HBM)
    send_pcs, pick = call(
        components_body,
        (pltpu.HBM((slots, npc), BF16), pltpu.HBM((obs, slots), BF16)),
        "components",
        in_hbm(spectra),
        in_hbm(pc_basis),
        place,
        specs=[hbm, hbm, vmem],
        outs=(hbm, hbm),
        scratch=[
            pltpu.VMEM((4, obs // 4, spectra.shape[1]), BF16),
            pltpu.VMEM((obs, npc), BF16),
            pltpu.VMEM((slots, obs), BF16),
            pltpu.VMEM((obs, slots), BF16),
            pltpu.VMEM((slots, npc), F32),
            pltpu.VMEM((slots, npc), BF16),
            pltpu.SemaphoreType.DMA((4,)),
            pltpu.SemaphoreType.DMA,
            pltpu.SemaphoreType.DMA((4,)),
            pltpu.VMEM(pc_basis.shape, BF16),
            pltpu.SemaphoreType.DMA,
        ],
        grant=42,
    )
    send_pcs, top, bottom, left, right = lax.optimization_barrier((send_pcs, top, bottom, left, right))
    recv_pcs = exchange(send_pcs.reshape(tiles, CAP, npc)).reshape(slots, npc)

    columns = call(
        gather_body,
        sds((slots, levels), BF16),
        "interpolate",
        recv_meta,
        state.reshape(-1, levels),
        top,
        bottom,
        left,
        right,
        scratch=[pltpu.VMEM((384, levels), BF16)] + [pltpu.VMEM((slots // 4, 4480), BF16)] * 4,
        grant=26,
    )
    dep, g = call(
        network_body,
        (pltpu.HBM((slots, npc), BF16), sds((slots, levels), BF16)),
        "network",
        columns,
        recv_pcs,
        inv_sigma[None],
        w_in,
        b_in[None],
        w_out,
        b_out[None],
        outs=(hbm, vmem),
        scratch=[pltpu.VMEM((slots, npc), BF16), pltpu.SemaphoreType.DMA((4,))],
        grant=16,
    )
    up, down, g_left, g_right = call(
        scatter_rim_body,
        (sds((64, levels), F32), sds((64, levels), F32), sds((80, levels), BF16), sds((80, levels), BF16)),
        "adjoint_rim",
        recv_meta,
        g,
        scratch=[pltpu.VMEM((288, slots), BF16)],
        grant=16,
    )
    from_right = shift(g_left, "lon", -1, True)
    from_left = shift(g_right, "lon", 1, True)
    back = exchange(dep.reshape(tiles, CAP, npc)).reshape(slots, npc)
    up, down = call(
        corner_body,
        (sds((64, levels), BF16), sds((64, levels), BF16)),
        "corners",
        up,
        down,
        from_left,
        from_right,
    )
    from_below = shift(up, "lat", -1, False)
    from_above = shift(down, "lat", 1, False)
    gradient = call(
        scatter_body,
        pltpu.HBM((64, 64, levels), F32),
        "adjoint",
        recv_meta,
        g,
        outs=hbm,
        scratch=[pltpu.VMEM((64, 64, levels), F32), pltpu.SemaphoreType.DMA((4,))]
        + [pltpu.VMEM((1024, slots), BF16)] * 4,
        grant=28,
    )
    departures, gradient = call(
        finish_body,
        (sds((obs, npc), BF16), pltpu.HBM((64, 64, levels), F32)),
        "finish",
        back,
        in_hbm(pick),
        from_left,
        from_right,
        from_above,
        from_below,
        in_hbm(gradient),
        specs=[vmem, hbm, vmem, vmem, vmem, vmem, hbm],
        outs=(vmem, hbm),
        scratch=[
            pltpu.VMEM((4, obs // 4, slots), BF16),
            pltpu.VMEM((2, 64, 8, levels), F32),
            pltpu.VMEM((2, 48, levels), F32),
            pltpu.SemaphoreType.DMA((4,)),
            pltpu.SemaphoreType.DMA((4,)),
            pltpu.SemaphoreType.DMA((4,)),
        ],
        alias={6: 1},
    )
    return (departures, gradient)


def solution(mesh):
    return jax.shard_map(
        per_device,
        mesh=mesh,
        in_specs=(
            P(AXES, None),
            P(),
            P(AXES, None),
            P(AXES),
            P(AXES),
            P(AXES, None),
            P("lat", "lon", None),
            P(),
            P(),
            P(),
            P(),
            P(),
        ),
        out_specs=(P(AXES, None), P("lat", "lon", None)),
        check_vma=False,
    )
```

```python
import functools

import jax
import jax.numpy as jnp
from jax import lax
from jax.experimental import pallas as pl
from jax.experimental.pallas import tpu as pltpu
from jax.sharding import PartitionSpec as P

CAP = 16
F32 = jnp.float32
BF16 = jnp.bfloat16
I32 = jnp.int32
NT = (((1,), (1,)), ((), ()))
AXES = ("lat", "lon")


def iota(shape, dim):
    return lax.broadcasted_iota(I32, shape, dim)


def mm(a, b):
    return jnp.dot(a, b, preferred_element_type=F32)


def ones_where(mask):
    return jnp.where(mask, 1.0, 0.0).astype(BF16)


def call(body, out_shape, name, *args, scratch=(), specs=None, outs=None, grant=8, alias=None):
    vmem = pl.BlockSpec(memory_space=pltpu.VMEM)
    return pl.pallas_call(
        body,
        in_specs=specs or [vmem] * len(args),
        out_specs=outs or jax.tree.map(lambda s: vmem, out_shape),
        out_shape=out_shape,
        scratch_shapes=scratch,
        input_output_aliases=alias or {},
        compiler_params=pltpu.CompilerParams(vmem_limit_bytes=grant << 20) if grant else None,
        name=name,
    )(*args)


def route_body(dest_ref, row_ref, col_ref, weight_ref, state_ref, send_ref, place_ref, first_ref, last_ref):
    first_ref[...] = state_ref[:, 0, :]
    last_ref[...] = state_ref[:, 63, :]
    dest = dest_ref[...]
    tiles = send_ref.shape[0]
    obs = dest.shape[1]
    onehot = jnp.where(iota((tiles, obs), 0) == dest, 1.0, 0.0)
    before = ones_where(iota((obs, obs), 0) < iota((obs, obs), 1))
    rank = mm(onehot.astype(BF16), before)
    slot = jnp.sum(onehot * rank, axis=0, keepdims=True).astype(I32)
    place_ref[...] = dest * CAP + slot
    here = iota((CAP, obs), 0) == slot
    weights = weight_ref[...].astype(F32)
    fields = [weights[k : k + 1] for k in range(4)]
    fields += [row_ref[...].astype(F32), col_ref[...].astype(F32)]
    parts = [jnp.where(here, field, 0.0) for field in fields]
    parts.append(jnp.zeros((128 - CAP * len(parts), obs), F32))
    table = jnp.concatenate(parts, 0).astype(BF16)
    send_ref[...] = lax.dot_general(onehot.astype(BF16), table, NT, preferred_element_type=F32)


def fields_by_row(recv, first, count):
    tiles = recv.shape[0]
    pick = ones_where((iota((count, tiles), 0) + first) // CAP == iota((count, tiles), 1))
    mine = mm(pick, recv)
    mine = jnp.where(iota((count, 128), 0) % CAP == iota((count, 128), 1) % CAP, mine, 0.0)
    spread = ones_where(iota((128, 768), 0) // CAP == iota((128, 768), 1) // 128)
    out = mm(mine.astype(BF16), spread)
    return [out[:, 128 * k : 128 * k + 128] for k in range(6)]


def fields_by_lane(recv, slots):
    tiles = recv.shape[0]
    pick = ones_where(iota((tiles, slots), 1) // CAP == iota((tiles, slots), 0))
    mine = mm(recv.astype(F32).T.astype(BF16), pick)
    mine = jnp.where(iota((128, slots), 1) % CAP == iota((128, slots), 0) % CAP, mine, 0.0)
    gather = ones_where(iota((8, 128), 1) // CAP == iota((8, 128), 0))
    out = mm(gather, mine.astype(BF16))
    return [out[k : k + 1] for k in range(6)]


def pair_of(hit0, value0, hit1, value1):
    return jnp.where(hit0, value0, jnp.where(hit1, value1, jnp.zeros((), value0.dtype)))


def gather_body(recv_ref, own_ref, top_ref, bottom_ref, left_ref, right_ref, out_ref, rim_ref, *matrices):
    slots = out_ref.shape[0]
    chunk = matrices[0].shape[0]
    rim_ref[0:64, :] = top_ref[...]
    rim_ref[64:128, :] = bottom_ref[...]
    rim_ref[128:192, :] = left_ref[0:64, :]
    rim_ref[192:256, :] = right_ref[0:64, :]
    rim_ref[256:272, :] = left_ref[64:80, :]
    rim_ref[272:288, :] = right_ref[64:80, :]
    rim_ref[288:384, :] = jnp.zeros((96, rim_ref.shape[1]), BF16)
    recv = recv_ref[...].astype(BF16)
    lane = iota((chunk, 128), 1).astype(F32)
    upper = jnp.where(lane >= 64.0, 1.0, 0.0)
    in_row = (lane - 64.0 * upper).astype(BF16)
    upper = upper.astype(BF16)
    lane = lane.astype(BF16)

    def build(first, matrix_ref):
        w0, w1, w2, w3, row, col = [f.astype(BF16) for f in fields_by_row(recv, first, chunk)]
        at0, at1 = in_row == col - 1.0, in_row == col
        p0 = pair_of(at0, w0, at1, w2)
        p1 = pair_of(at0, w1, at1, w3)
        zero = jnp.zeros((), BF16)
        edge = 65.0 * upper
        matrix_ref[:, 4096:4224] = pair_of(edge == row, p0, edge == row + 1.0, p1)
        high = upper > 0.5
        side = pair_of(in_row == row - 1.0, jnp.where(high, w2, w0), in_row == row, jnp.where(high, w3, w1))
        matrix_ref[:, 4224:4352] = jnp.where(col == 64.0 * upper, side, zero)
        corner = pair_of(lane == 0.0, w0, lane == 1.0, w1) + pair_of(lane == 16.0, w2, lane == 17.0, w3)
        at_col = jnp.where(lane < 16.0, zero, zero + 64.0)
        odd = jnp.where(lane < 16.0, lane, lane - 16.0)
        matrix_ref[:, 4352:4480] = jnp.where(row == 64.0 * odd, jnp.where(col == at_col, corner, zero), zero)
        offset = row - upper
        for j in range(32):
            matrix_ref[:, 128 * j : 128 * j + 128] = pair_of(offset == 2.0 * j + 1.0, p0, offset == 2.0 * j, p1)

    def use(first, matrix_ref):
        out = mm(matrix_ref[:, :4096], own_ref[...]) + mm(matrix_ref[:, 4096:], rim_ref[...])
        out_ref[first : first + chunk, :] = out.astype(BF16)

    count = slots // chunk
    build(0, matrices[0])
    for i in range(count):
        if i + 1 < count:
            build((i + 1) * chunk, matrices[i + 1])
        use(i * chunk, matrices[i])


def components_body(spectra_ref, basis_ref, place_ref, pcs_ref, buffer, basis_buffer, sems, basis_sem):
    obs = spectra_ref.shape[0]
    blocks = buffer.shape[0]
    rows = obs // blocks
    basis = pltpu.make_async_copy(basis_ref, basis_buffer, basis_sem)
    basis.start()
    copies = [
        pltpu.make_async_copy(spectra_ref.at[pl.ds(i * rows, rows), :], buffer.at[i], sems.at[i]) for i in range(blocks)
    ]
    for copy in copies:
        copy.start()
    basis.wait()
    for i, copy in enumerate(copies):
        copy.wait()
        pcs_ref[i * rows : i * rows + rows, :] = mm(buffer[i], basis_buffer[...]).astype(BF16)


def network_body(recv_ref, place_ref, pcs_ref, inv_ref, w_in_hbm, b_in_ref, w_out_hbm, b_out_ref, dep_ref, send_ref, pack_ref, unpack_ref, w_in_ref, w_out_ref, g_ref, dep_buffer, send_buffer, w_sems, dep_sems, send_sems):
    slots = recv_ref.shape[0]
    obs = pcs_ref.shape[0]
    loads = [pltpu.make_async_copy(w_in_hbm, w_in_ref, w_sems.at[0]), pltpu.make_async_copy(w_out_hbm, w_out_ref, w_sems.at[1])]
    for copy in loads:
        copy.start()
    inv = inv_ref[...]
    copies = []
    block = obs // 4
    place = place_ref[...]
    wide = jnp.broadcast_to(place.astype(F32), (128, obs)).T
    lane = iota((block, 128), 1).astype(F32)
    for i in range(4):
        at = slice(i * block, (i + 1) * block)
        for b in range(slots // 128):
            unpack_ref[at, 128 * b : 128 * b + 128] = ones_where(wide[at] - 128.0 * b == lane)
        half = slots // 4
        pack_ref[i * half : (i + 1) * half, :] = ones_where(iota((half, obs), 0) + i * half == place)
        column = mm(unpack_ref[at, :], recv_ref[...]).astype(BF16)
        if i == 0:
            for copy in loads:
                copy.wait()
        pre = mm(column, w_in_ref[...]) + b_in_ref[...]
        sig = jax.nn.sigmoid(pre)
        hidden = (pre * sig).astype(BF16)
        sim = mm(hidden, w_out_ref[...]) + b_out_ref[...]
        dep = (sim - pcs_ref[at, :].astype(F32)) * inv
        dep_buffer[at, :] = dep.astype(BF16)
        copies.append(pltpu.make_async_copy(dep_buffer.at[at, :], dep_ref.at[at, :], dep_sems.at[i]))
        copies[-1].start()
        g_sim = (dep * inv).astype(BF16)
        g_hidden = lax.dot_general(g_sim, w_out_ref[...], NT, preferred_element_type=F32)
        g_pre = (g_hidden * sig * (1.0 + pre * (1.0 - sig))).astype(BF16)
        g_ref[at, :] = lax.dot_general(g_pre, w_in_ref[...], NT, preferred_element_type=F32).astype(BF16)
    block = slots // 4
    for i in range(4):
        at = slice(i * block, (i + 1) * block)
        send_buffer[at, :] = mm(pack_ref[at, :], g_ref[...]).astype(BF16)
        copies.append(pltpu.make_async_copy(send_buffer.at[at, :], send_ref.at[at, :], send_sems.at[i]))
        copies[-1].start()
    for copy in copies:
        copy.wait()


def prepare_body(recv_ref, fields_ref):
    fields = fields_by_lane(recv_ref[...].astype(BF16), fields_ref.shape[1])
    fields_ref[...] = jnp.concatenate(fields + [fields[5], fields[5]], 0)


def scatter_rim_body(fields_ref, g_ref, up_ref, down_ref, left_ref, right_ref, rim_ref):
    slots = g_ref.shape[0]
    w0, w1, w2, w3, row, col = [fields_ref[k : k + 1, :].astype(BF16) for k in range(6)]
    zero = jnp.zeros((), BF16)
    sub = iota((64, slots), 0).astype(F32).astype(BF16)
    at0, at1 = sub == row - 1.0, sub == row
    rim_ref[128:192, :] = jnp.where(col == 0.0, pair_of(at0, w0, at1, w1), zero)
    rim_ref[208:272, :] = jnp.where(col == 64.0, pair_of(at0, w2, at1, w3), zero)
    low = iota((16, slots), 0).astype(F32).astype(BF16)
    first, last = jnp.where(row == 0.0, zero, zero - 1.0), jnp.where(row == 64.0, zero + 1.0, zero - 1.0)
    rim_ref[192:208, :] = jnp.where(col == 0.0, pair_of(low == first, w0, low == last, w1), zero)
    rim_ref[272:288, :] = jnp.where(col == 64.0, pair_of(low == first, w2, low == last, w3), zero)
    at0, at1 = sub == col - 1.0, sub == col
    rim_ref[0:64, :] = jnp.where(row == 0.0, pair_of(at0, w0, at1, w2), zero)
    rim_ref[64:128, :] = jnp.where(row == 64.0, pair_of(at0, w1, at1, w3), zero)
    out = mm(rim_ref[...], g_ref[...])
    up_ref[...] = out[0:64]
    down_ref[...] = out[64:128]
    left_ref[...] = out[128:208].astype(BF16)
    right_ref[...] = out[208:288].astype(BF16)


def corner_body(up_ref, down_ref, left_ref, right_ref, up_out, down_out):
    at = iota((64, 128), 0)
    left = left_ref[64:80, :].astype(F32)
    right = right_ref[64:80, :].astype(F32)
    for k, (ref, out) in enumerate(((up_ref, up_out), (down_ref, down_out))):
        extra = jnp.where(at == 0, left[k : k + 1], jnp.where(at == 63, right[k : k + 1], 0.0))
        out[...] = (ref[...] + extra).astype(BF16)


def scatter_body(half, fields_ref, g_ref, *refs):
    out_ref, buffer, sems = refs[-5:-2]
    matrices = refs[-2:]
    slots = g_ref.shape[0]
    rows = 16
    w0, w1, w2, w3, row, col = [fields_ref[k : k + 1, :].astype(BF16) for k in range(6)]
    sub = iota((64, slots), 0).astype(F32).astype(BF16)
    at0, at1 = sub == col - 1.0, sub == col
    p0 = pair_of(at0, w0, at1, w2)
    p1 = pair_of(at0, w1, at1, w3)
    row = jnp.broadcast_to(row, (64, slots))

    def build(first, matrix_ref):
        for j in range(rows):
            at = float(first + j)
            matrix_ref[64 * j : 64 * j + 64, :] = pair_of(row == at + 1.0, p0, row == at, p1)

    copies = []
    build(32 * half, matrices[0])
    for i in range(2):
        first = 32 * half + rows * i
        if i == 0:
            build(first + rows, matrices[1])
        out = mm(matrices[i][...], g_ref[...])
        buffer[i] = out.reshape(rows, 64, out.shape[1])
        copies.append(pltpu.make_async_copy(buffer.at[i], out_ref.at[pl.ds(first, rows)], sems.at[i]))
        copies[i].start()
    for copy in copies:
        copy.wait()


def edge_body(left_ref, right_ref, above_ref, below_ref, grad_ref, out_ref, sides, rows, in_sems, out_sems):
    edges = [
        (out_ref.at[:, pl.ds(0, 8), :], sides.at[0]),
        (out_ref.at[:, pl.ds(56, 8), :], sides.at[1]),
        (out_ref.at[0, pl.ds(8, 48), :], rows.at[0]),
        (out_ref.at[63, pl.ds(8, 48), :], rows.at[1]),
    ]
    loads = [pltpu.make_async_copy(a, b, in_sems.at[i]) for i, (a, b) in enumerate(edges)]
    stores = [pltpu.make_async_copy(b, a, out_sems.at[i]) for i, (a, b) in enumerate(edges)]
    for copy in loads:
        copy.start()
    for copy in loads:
        copy.wait()
    above, below = above_ref[...].astype(F32), below_ref[...].astype(F32)
    sides[0, :, 0, :] += left_ref[0:64, :].astype(F32)
    sides[1, :, 7, :] += right_ref[0:64, :].astype(F32)
    sides[0, 0] += above[0:8]
    sides[1, 0] += above[56:64]
    sides[0, 63] += below[0:8]
    sides[1, 63] += below[56:64]
    rows[0] += above[8:56]
    rows[1] += below[8:56]
    for copy in stores:
        copy.start()
    for copy in stores:
        copy.wait()


def in_hbm(x):
    return pltpu.with_memory_space_constraint(x, pltpu.HBM)


def shift(x, axis, step, closed):
    count = lax.axis_size(axis)
    pairs = [(i, (i + step) % count) for i in range(count) if closed or 0 <= i + step < count]
    return lax.ppermute(x, axis, pairs)


def exchange(x):
    return lax.all_to_all(x, AXES, split_axis=0, concat_axis=0, tiled=True)


def per_device(
    spectra,
    pc_basis,
    destination,
    corner_row,
    corner_col,
    corner_weight,
    state,
    inv_sigma,
    w_in,
    b_in,
    w_out,
    b_out,
):
    tiles = lax.axis_size("lat") * lax.axis_size("lon")
    obs = spectra.shape[0]
    npc = pc_basis.shape[1]
    levels = state.shape[2]
    slots = tiles * CAP
    sds = jax.ShapeDtypeStruct

    top = shift(state[63], "lat", 1, False)
    bottom = shift(state[0], "lat", -1, False)
    send_meta, place, first, last = call(
        route_body,
        (sds((tiles, 128), F32), sds((1, obs), I32), sds((64, levels), BF16), sds((64, levels), BF16)),
        "route",
        destination.reshape(1, obs),
        corner_row.reshape(1, obs),
        corner_col.reshape(1, obs),
        corner_weight.T,
        state,
        grant=None,
    )
    recv_meta = exchange(send_meta)

    fill = jnp.zeros((14, levels), BF16)
    left = shift(jnp.concatenate([last, top[63:], bottom[63:], fill], 0), "lon", 1, True)
    right = shift(jnp.concatenate([first, top[:1], bottom[:1], fill], 0), "lon", -1, True)

    vmem = pl.BlockSpec(memory_space=pltpu.VMEM)
    hbm = pl.BlockSpec(memory_space=pltpu.HBM)
    columns = call(
        gather_body,
        pltpu.HBM((slots, levels), BF16),
        "interpolate",
        recv_meta,
        state.reshape(-1, levels),
        top,
        bottom,
        left,
        right,
        scratch=[pltpu.VMEM((384, levels), BF16)] + [pltpu.VMEM((slots // 4, 4480), BF16)] * 4,
        grant=26,
    )
    columns, place = lax.optimization_barrier((columns, place))
    recv_columns = exchange(columns.reshape(tiles, CAP, levels)).reshape(slots, levels)
    pcs = call(
        components_body,
        sds((obs, npc), BF16),
        "components",
        in_hbm(spectra),
        in_hbm(pc_basis),
        place,
        specs=[hbm, hbm, vmem],
        scratch=[
            pltpu.VMEM((4, obs // 4, spectra.shape[1]), BF16),
            pltpu.VMEM(pc_basis.shape, BF16),
            pltpu.SemaphoreType.DMA((4,)),
            pltpu.SemaphoreType.DMA,
        ],
        grant=26,
    )
    departures, send_g = call(
        network_body,
        (pltpu.HBM((obs, npc), BF16), pltpu.HBM((slots, levels), BF16)),
        "network",
        recv_columns,
        place,
        pcs,
        inv_sigma[None],
        in_hbm(w_in),
        b_in[None],
        in_hbm(w_out),
        b_out[None],
        specs=[vmem] * 4 + [hbm, vmem, hbm, vmem],
        outs=(hbm, hbm),
        scratch=[
            pltpu.VMEM((slots, obs), BF16),
            pltpu.VMEM((obs, slots), BF16),
            pltpu.VMEM(w_in.shape, BF16),
            pltpu.VMEM(w_out.shape, BF16),
            pltpu.VMEM((obs, levels), BF16),
            pltpu.VMEM((obs, npc), BF16),
            pltpu.VMEM((slots, levels), BF16),
            pltpu.SemaphoreType.DMA((2,)),
            pltpu.SemaphoreType.DMA((4,)),
            pltpu.SemaphoreType.DMA((4,)),
        ],
        grant=24,
    )
    send_g, recv_meta = lax.optimization_barrier((send_g, recv_meta))
    g = exchange(send_g.reshape(tiles, CAP, levels)).reshape(slots, levels)
    fields = call(prepare_body, sds((8, slots), F32), "prepare", recv_meta)
    up, down, g_left, g_right = call(
        scatter_rim_body,
        (sds((64, levels), F32), sds((64, levels), F32), sds((80, levels), BF16), sds((80, levels), BF16)),
        "adjoint_rim",
        fields,
        g,
        scratch=[pltpu.VMEM((288, slots), BF16)],
    )
    from_right = shift(g_left, "lon", -1, True)
    from_left = shift(g_right, "lon", 1, True)
    half = [pltpu.VMEM((2, 16, 64, levels), F32), pltpu.SemaphoreType.DMA((2,))]
    half += [pltpu.VMEM((1024, slots), BF16)] * 2
    gradient = call(
        functools.partial(scatter_body, 0),
        pltpu.HBM((64, 64, levels), F32),
        "adjoint_a",
        fields,
        g,
        outs=hbm,
        scratch=half,
        grant=14,
    )
    up, down = call(
        corner_body,
        (sds((64, levels), BF16), sds((64, levels), BF16)),
        "corners",
        up,
        down,
        from_left,
        from_right,
    )
    up, down, g = lax.optimization_barrier((up, down, g))
    from_below = shift(up, "lat", -1, False)
    from_above = shift(down, "lat", 1, False)
    gradient = call(
        functools.partial(scatter_body, 1),
        pltpu.HBM((64, 64, levels), F32),
        "adjoint_b",
        fields,
        g,
        in_hbm(gradient),
        specs=[vmem, vmem, hbm],
        outs=hbm,
        scratch=half,
        grant=14,
        alias={2: 0},
    )
    gradient = call(
        edge_body,
        pltpu.HBM((64, 64, levels), F32),
        "edges",
        from_left,
        from_right,
        from_above,
        from_below,
        in_hbm(gradient),
        specs=[vmem, vmem, vmem, vmem, hbm],
        outs=hbm,
        scratch=[
            pltpu.VMEM((2, 64, 8, levels), F32),
            pltpu.VMEM((2, 48, levels), F32),
            pltpu.SemaphoreType.DMA((4,)),
            pltpu.SemaphoreType.DMA((4,)),
        ],
        alias={4: 0},
    )
    return (departures, gradient)


def solution(mesh):
    return jax.shard_map(
        per_device,
        mesh=mesh,
        in_specs=(
            P(AXES, None),
            P(),
            P(AXES, None),
            P(AXES),
            P(AXES),
            P(AXES, None),
            P("lat", "lon", None),
            P(),
            P(),
            P(),
            P(),
            P(),
        ),
        out_specs=(P(AXES, None), P("lat", "lon", None)),
        check_vma=False,
    )
```

```python
import functools

import jax
import jax.numpy as jnp
from jax import lax
from jax.experimental import pallas as pl
from jax.experimental.pallas import tpu as pltpu
from jax.sharding import PartitionSpec as P

CAP = 16
F32 = jnp.float32
BF16 = jnp.bfloat16
I32 = jnp.int32
NT = (((1,), (1,)), ((), ()))
AXES = ("lat", "lon")


def iota(shape, dim):
    return lax.broadcasted_iota(I32, shape, dim)


def mm(a, b):
    return jnp.dot(a, b, preferred_element_type=F32)


def ones_where(mask):
    return jnp.where(mask, 1.0, 0.0).astype(BF16)


def call(body, out_shape, name, *args, scratch=(), specs=None, outs=None, grant=8, alias=None):
    vmem = pl.BlockSpec(memory_space=pltpu.VMEM)
    return pl.pallas_call(
        body,
        in_specs=specs or [vmem] * len(args),
        out_specs=outs or jax.tree.map(lambda s: vmem, out_shape),
        out_shape=out_shape,
        scratch_shapes=scratch,
        input_output_aliases=alias or {},
        compiler_params=pltpu.CompilerParams(vmem_limit_bytes=grant << 20) if grant else None,
        name=name,
    )(*args)


def route_body(dest_ref, row_ref, col_ref, weight_ref, state_ref, send_ref, place_ref, first_ref, last_ref, head_ref, tail_ref):
    first_ref[...] = state_ref[:, 0, :]
    last_ref[...] = state_ref[:, 63, :]
    head_ref[...] = state_ref[0]
    tail_ref[...] = state_ref[63]
    dest = dest_ref[...]
    tiles = send_ref.shape[0]
    obs = dest.shape[1]
    onehot = jnp.where(iota((tiles, obs), 0) == dest, 1.0, 0.0)
    before = ones_where(iota((obs, obs), 0) < iota((obs, obs), 1))
    rank = mm(onehot.astype(BF16), before)
    slot = jnp.sum(onehot * rank, axis=0, keepdims=True).astype(I32)
    place_ref[...] = dest * CAP + slot
    here = iota((CAP, obs), 0) == slot
    weights = weight_ref[...].astype(F32)
    fields = [weights[k : k + 1] for k in range(4)]
    fields += [row_ref[...].astype(F32), col_ref[...].astype(F32)]
    parts = [jnp.where(here, field, 0.0) for field in fields]
    parts.append(jnp.zeros((128 - CAP * len(parts), obs), F32))
    table = jnp.concatenate(parts, 0).astype(BF16)
    send_ref[...] = lax.dot_general(onehot.astype(BF16), table, NT, preferred_element_type=F32)


def fields_by_row(recv, first, count):
    tiles = recv.shape[0]
    pick = ones_where((iota((count, tiles), 0) + first) // CAP == iota((count, tiles), 1))
    mine = mm(pick, recv)
    mine = jnp.where(iota((count, 128), 0) % CAP == iota((count, 128), 1) % CAP, mine, 0.0)
    spread = ones_where(iota((128, 768), 0) // CAP == iota((128, 768), 1) // 128)
    out = mm(mine.astype(BF16), spread)
    return [out[:, 128 * k : 128 * k + 128] for k in range(6)]


def fields_by_lane(recv, slots):
    tiles = recv.shape[0]
    pick = ones_where(iota((tiles, slots), 1) // CAP == iota((tiles, slots), 0))
    mine = mm(recv.astype(F32).T.astype(BF16), pick)
    mine = jnp.where(iota((128, slots), 1) % CAP == iota((128, slots), 0) % CAP, mine, 0.0)
    gather = ones_where(iota((8, 128), 1) // CAP == iota((8, 128), 0))
    out = mm(gather, mine.astype(BF16))
    return [out[k : k + 1] for k in range(6)]


def pair_of(hit0, value0, hit1, value1):
    return jnp.where(hit0, value0, jnp.where(hit1, value1, jnp.zeros((), value0.dtype)))


def gather_body(recv_ref, own_ref, top_ref, bottom_ref, left_ref, right_ref, out_ref, rim_ref, *matrices):
    slots = out_ref.shape[0]
    chunk = matrices[0].shape[0]
    rim_ref[0:64, :] = top_ref[...]
    rim_ref[64:128, :] = bottom_ref[...]
    rim_ref[128:192, :] = left_ref[0:64, :]
    rim_ref[192:256, :] = right_ref[0:64, :]
    rim_ref[256:272, :] = left_ref[64:80, :]
    rim_ref[272:288, :] = right_ref[64:80, :]
    rim_ref[288:384, :] = jnp.zeros((96, rim_ref.shape[1]), BF16)
    recv = recv_ref[...].astype(BF16)
    lane = iota((chunk, 128), 1).astype(F32)
    upper = jnp.where(lane >= 64.0, 1.0, 0.0)
    in_row = (lane - 64.0 * upper).astype(BF16)
    upper = upper.astype(BF16)
    lane = lane.astype(BF16)

    def build(first, matrix_ref):
        w0, w1, w2, w3, row, col = [f.astype(BF16) for f in fields_by_row(recv, first, chunk)]
        at0, at1 = in_row == col - 1.0, in_row == col
        p0 = pair_of(at0, w0, at1, w2)
        p1 = pair_of(at0, w1, at1, w3)
        zero = jnp.zeros((), BF16)
        edge = 65.0 * upper
        matrix_ref[:, 4096:4224] = pair_of(edge == row, p0, edge == row + 1.0, p1)
        high = upper > 0.5
        side = pair_of(in_row == row - 1.0, jnp.where(high, w2, w0), in_row == row, jnp.where(high, w3, w1))
        matrix_ref[:, 4224:4352] = jnp.where(col == 64.0 * upper, side, zero)
        corner = pair_of(lane == 0.0, w0, lane == 1.0, w1) + pair_of(lane == 16.0, w2, lane == 17.0, w3)
        at_col = jnp.where(lane < 16.0, zero, zero + 64.0)
        odd = jnp.where(lane < 16.0, lane, lane - 16.0)
        matrix_ref[:, 4352:4480] = jnp.where(row == 64.0 * odd, jnp.where(col == at_col, corner, zero), zero)
        offset = row - upper
        for j in range(32):
            matrix_ref[:, 128 * j : 128 * j + 128] = pair_of(offset == 2.0 * j + 1.0, p0, offset == 2.0 * j, p1)

    def use(first, matrix_ref):
        out = mm(matrix_ref[:, :4096], own_ref[...]) + mm(matrix_ref[:, 4096:], rim_ref[...])
        out_ref[first : first + chunk, :] = out.astype(BF16)

    count = slots // chunk
    build(0, matrices[0])
    for i in range(count):
        if i + 1 < count:
            build((i + 1) * chunk, matrices[i + 1])
        use(i * chunk, matrices[i])


def components_body(spectra_ref, basis_ref, place_ref, pcs_ref, buffer, basis_buffer, sems, basis_sem):
    obs = spectra_ref.shape[0]
    blocks = buffer.shape[0]
    rows = obs // blocks

    def load(i):
        at = pl.ds(pl.multiple_of(i * rows, rows), rows)
        return pltpu.make_async_copy(spectra_ref.at[at, :], buffer.at[i], sems.at[i])

    basis = pltpu.make_async_copy(basis_ref, basis_buffer, basis_sem)
    basis.start()
    load(0).start()
    load(1).start()
    basis.wait()

    def step(i, carry):
        load(i).wait()

        @pl.when(i + 2 < blocks)
        def _():
            load(i + 2).start()

        at = pl.ds(pl.multiple_of(i * rows, rows), rows)
        pcs_ref[at, :] = mm(buffer[i], basis_buffer[...]).astype(BF16)
        return carry

    lax.fori_loop(0, blocks, step, 0)


def network_body(recv_ref, place_ref, pcs_ref, inv_ref, w_in_hbm, b_in_ref, w_out_hbm, b_out_ref, dep_ref, send_ref, pack_ref, unpack_ref, w_in_ref, w_out_ref, g_ref, dep_buffer, send_buffer, w_sems, dep_sems, send_sems):
    slots = recv_ref.shape[0]
    obs = pcs_ref.shape[0]
    loads = [pltpu.make_async_copy(w_in_hbm, w_in_ref, w_sems.at[0]), pltpu.make_async_copy(w_out_hbm, w_out_ref, w_sems.at[1])]
    for copy in loads:
        copy.start()
    inv = inv_ref[...]
    copies = []
    block = obs // 4
    place = place_ref[...]
    wide = jnp.broadcast_to(place.astype(F32), (128, obs)).T
    lane = iota((block, 128), 1).astype(F32)
    for i in range(4):
        at = slice(i * block, (i + 1) * block)
        for b in range(slots // 128):
            unpack_ref[at, 128 * b : 128 * b + 128] = ones_where(wide[at] - 128.0 * b == lane)
        half = slots // 4
        pack_ref[i * half : (i + 1) * half, :] = ones_where(iota((half, obs), 0) + i * half == place)
        column = mm(unpack_ref[at, :], recv_ref[...]).astype(BF16)
        if i == 0:
            for copy in loads:
                copy.wait()
        pre = mm(column, w_in_ref[...]) + b_in_ref[...]
        sig = jax.nn.sigmoid(pre)
        hidden = (pre * sig).astype(BF16)
        sim = mm(hidden, w_out_ref[...]) + b_out_ref[...]
        dep = (sim - pcs_ref[at, :].astype(F32)) * inv
        dep_buffer[at, :] = dep.astype(BF16)
        copies.append(pltpu.make_async_copy(dep_buffer.at[at, :], dep_ref.at[at, :], dep_sems.at[i]))
        copies[-1].start()
        g_sim = (dep * inv).astype(BF16)
        g_hidden = lax.dot_general(g_sim, w_out_ref[...], NT, preferred_element_type=F32)
        g_pre = (g_hidden * sig * (1.0 + pre * (1.0 - sig))).astype(BF16)
        g_ref[at, :] = lax.dot_general(g_pre, w_in_ref[...], NT, preferred_element_type=F32).astype(BF16)
    block = slots // 4
    for i in range(4):
        at = slice(i * block, (i + 1) * block)
        send_buffer[at, :] = mm(pack_ref[at, :], g_ref[...]).astype(BF16)
        copies.append(pltpu.make_async_copy(send_buffer.at[at, :], send_ref.at[at, :], send_sems.at[i]))
        copies[-1].start()
    for copy in copies:
        copy.wait()


def prepare_body(recv_ref, fields_ref):
    fields = fields_by_lane(recv_ref[...].astype(BF16), fields_ref.shape[1])
    fields_ref[...] = jnp.concatenate(fields + [fields[5], fields[5]], 0)


def scatter_rim_body(fields_ref, g_ref, up_ref, down_ref, left_ref, right_ref, rim_ref):
    slots = g_ref.shape[0]
    w0, w1, w2, w3, row, col = [fields_ref[k : k + 1, :].astype(BF16) for k in range(6)]
    zero = jnp.zeros((), BF16)
    sub = iota((64, slots), 0).astype(F32).astype(BF16)
    at0, at1 = sub == row - 1.0, sub == row
    rim_ref[128:192, :] = jnp.where(col == 0.0, pair_of(at0, w0, at1, w1), zero)
    rim_ref[208:272, :] = jnp.where(col == 64.0, pair_of(at0, w2, at1, w3), zero)
    low = iota((16, slots), 0).astype(F32).astype(BF16)
    first, last = jnp.where(row == 0.0, zero, zero - 1.0), jnp.where(row == 64.0, zero + 1.0, zero - 1.0)
    rim_ref[192:208, :] = jnp.where(col == 0.0, pair_of(low == first, w0, low == last, w1), zero)
    rim_ref[272:288, :] = jnp.where(col == 64.0, pair_of(low == first, w2, low == last, w3), zero)
    at0, at1 = sub == col - 1.0, sub == col
    rim_ref[0:64, :] = jnp.where(row == 0.0, pair_of(at0, w0, at1, w2), zero)
    rim_ref[64:128, :] = jnp.where(row == 64.0, pair_of(at0, w1, at1, w3), zero)
    out = mm(rim_ref[...], g_ref[...])
    up_ref[...] = out[0:64]
    down_ref[...] = out[64:128]
    left_ref[...] = out[128:208].astype(BF16)
    right_ref[...] = out[208:288].astype(BF16)


def corner_body(up_ref, down_ref, left_ref, right_ref, up_out, down_out):
    at = iota((64, 128), 0)
    left = left_ref[64:80, :].astype(F32)
    right = right_ref[64:80, :].astype(F32)
    for k, (ref, out) in enumerate(((up_ref, up_out), (down_ref, down_out))):
        extra = jnp.where(at == 0, left[k : k + 1], jnp.where(at == 63, right[k : k + 1], 0.0))
        out[...] = (ref[...] + extra).astype(BF16)


def scatter_body(half, fields_ref, g_ref, *refs):
    out_ref, buffer, sems = refs[-5:-2]
    matrices = refs[-2:]
    slots = g_ref.shape[0]
    rows = 16
    w0, w1, w2, w3, row, col = [fields_ref[k : k + 1, :].astype(BF16) for k in range(6)]
    sub = iota((64, slots), 0).astype(F32).astype(BF16)
    at0, at1 = sub == col - 1.0, sub == col
    p0 = pair_of(at0, w0, at1, w2)
    p1 = pair_of(at0, w1, at1, w3)
    row = jnp.broadcast_to(row, (64, slots))

    def build(first, matrix_ref):
        for j in range(rows):
            at = float(first + j)
            matrix_ref[64 * j : 64 * j + 64, :] = pair_of(row == at + 1.0, p0, row == at, p1)

    copies = []
    build(32 * half, matrices[0])
    for i in range(2):
        first = 32 * half + rows * i
        if i == 0:
            build(first + rows, matrices[1])
        out = mm(matrices[i][...], g_ref[...])
        buffer[i] = out.reshape(rows, 64, out.shape[1])
        copies.append(pltpu.make_async_copy(buffer.at[i], out_ref.at[pl.ds(first, rows)], sems.at[i]))
        copies[i].start()
    for copy in copies:
        copy.wait()


def edge_body(left_ref, right_ref, above_ref, below_ref, grad_ref, out_ref, sides, rows, in_sems, out_sems):
    edges = [
        (out_ref.at[:, pl.ds(0, 8), :], sides.at[0]),
        (out_ref.at[:, pl.ds(56, 8), :], sides.at[1]),
        (out_ref.at[0, pl.ds(8, 48), :], rows.at[0]),
        (out_ref.at[63, pl.ds(8, 48), :], rows.at[1]),
    ]
    loads = [pltpu.make_async_copy(a, b, in_sems.at[i]) for i, (a, b) in enumerate(edges)]
    stores = [pltpu.make_async_copy(b, a, out_sems.at[i]) for i, (a, b) in enumerate(edges)]
    for copy in loads:
        copy.start()
    for copy in loads:
        copy.wait()
    above, below = above_ref[...].astype(F32), below_ref[...].astype(F32)
    sides[0, :, 0, :] += left_ref[0:64, :].astype(F32)
    sides[1, :, 7, :] += right_ref[0:64, :].astype(F32)
    sides[0, 0] += above[0:8]
    sides[1, 0] += above[56:64]
    sides[0, 63] += below[0:8]
    sides[1, 63] += below[56:64]
    rows[0] += above[8:56]
    rows[1] += below[8:56]
    for copy in stores:
        copy.start()
    for copy in stores:
        copy.wait()


def in_hbm(x):
    return pltpu.with_memory_space_constraint(x, pltpu.HBM)


def shift(x, axis, step, closed):
    count = lax.axis_size(axis)
    pairs = [(i, (i + step) % count) for i in range(count) if closed or 0 <= i + step < count]
    return lax.ppermute(x, axis, pairs)


def exchange(x):
    return lax.all_to_all(x, AXES, split_axis=0, concat_axis=0, tiled=True)


def per_device(
    spectra,
    pc_basis,
    destination,
    corner_row,
    corner_col,
    corner_weight,
    state,
    inv_sigma,
    w_in,
    b_in,
    w_out,
    b_out,
):
    tiles = lax.axis_size("lat") * lax.axis_size("lon")
    obs = spectra.shape[0]
    npc = pc_basis.shape[1]
    levels = state.shape[2]
    slots = tiles * CAP
    sds = jax.ShapeDtypeStruct

    send_meta, place, first, last, head, tail = call(
        route_body,
        (pltpu.HBM((tiles, 128), F32), sds((1, obs), I32)) + (sds((64, levels), BF16),) * 4,
        "route",
        destination.reshape(1, obs),
        corner_row.reshape(1, obs),
        corner_col.reshape(1, obs),
        corner_weight.T,
        state,
        grant=None,
    )
    recv_meta = exchange(send_meta)
    top = shift(tail, "lat", 1, False)
    bottom = shift(head, "lat", -1, False)
    fill = jnp.zeros((14, levels), BF16)
    left = shift(jnp.concatenate([last, top[63:], bottom[63:], fill], 0), "lon", 1, True)
    right = shift(jnp.concatenate([first, top[:1], bottom[:1], fill], 0), "lon", -1, True)

    vmem = pl.BlockSpec(memory_space=pltpu.VMEM)
    hbm = pl.BlockSpec(memory_space=pltpu.HBM)
    columns = call(
        gather_body,
        pltpu.HBM((slots, levels), BF16),
        "interpolate",
        recv_meta,
        state.reshape(-1, levels),
        top,
        bottom,
        left,
        right,
        scratch=[pltpu.VMEM((384, levels), BF16)] + [pltpu.VMEM((slots // 4, 4480), BF16)] * 4,
        grant=26,
    )
    columns, place = lax.optimization_barrier((columns, place))
    recv_columns = exchange(columns.reshape(tiles, CAP, levels)).reshape(slots, levels)
    pcs = call(
        components_body,
        sds((obs, npc), BF16),
        "components",
        in_hbm(spectra),
        in_hbm(pc_basis),
        place,
        specs=[hbm, hbm, vmem],
        scratch=[
            pltpu.VMEM((4, obs // 4, spectra.shape[1]), BF16),
            pltpu.VMEM(pc_basis.shape, BF16),
            pltpu.SemaphoreType.DMA((4,)),
            pltpu.SemaphoreType.DMA,
        ],
        grant=26,
    )
    departures, send_g = call(
        network_body,
        (pltpu.HBM((obs, npc), BF16), pltpu.HBM((slots, levels), BF16)),
        "network",
        recv_columns,
        place,
        pcs,
        inv_sigma[None],
        in_hbm(w_in),
        b_in[None],
        in_hbm(w_out),
        b_out[None],
        specs=[vmem] * 4 + [hbm, vmem, hbm, vmem],
        outs=(hbm, hbm),
        scratch=[
            pltpu.VMEM((slots, obs), BF16),
            pltpu.VMEM((obs, slots), BF16),
            pltpu.VMEM(w_in.shape, BF16),
            pltpu.VMEM(w_out.shape, BF16),
            pltpu.VMEM((obs, levels), BF16),
            pltpu.VMEM((obs, npc), BF16),
            pltpu.VMEM((slots, levels), BF16),
            pltpu.SemaphoreType.DMA((2,)),
            pltpu.SemaphoreType.DMA((4,)),
            pltpu.SemaphoreType.DMA((4,)),
        ],
        grant=24,
    )
    send_g, recv_meta = lax.optimization_barrier((send_g, recv_meta))
    g = exchange(send_g.reshape(tiles, CAP, levels)).reshape(slots, levels)
    fields = call(prepare_body, sds((8, slots), F32), "prepare", recv_meta)
    up, down, g_left, g_right = call(
        scatter_rim_body,
        (sds((64, levels), F32), sds((64, levels), F32), sds((80, levels), BF16), sds((80, levels), BF16)),
        "adjoint_rim",
        fields,
        g,
        scratch=[pltpu.VMEM((288, slots), BF16)],
    )
    from_right = shift(g_left, "lon", -1, True)
    from_left = shift(g_right, "lon", 1, True)
    half = [pltpu.VMEM((2, 16, 64, levels), F32), pltpu.SemaphoreType.DMA((2,))]
    half += [pltpu.VMEM((1024, slots), BF16)] * 2
    gradient = call(
        functools.partial(scatter_body, 0),
        pltpu.HBM((64, 64, levels), F32),
        "adjoint_a",
        fields,
        g,
        outs=hbm,
        scratch=half,
        grant=14,
    )
    from_left, from_right, gradient = lax.optimization_barrier((from_left, from_right, gradient))
    up, down = call(
        corner_body,
        (sds((64, levels), BF16), sds((64, levels), BF16)),
        "corners",
        up,
        down,
        from_left,
        from_right,
    )
    up, down, g = lax.optimization_barrier((up, down, g))
    from_below = shift(up, "lat", -1, False)
    from_above = shift(down, "lat", 1, False)
    gradient = call(
        functools.partial(scatter_body, 1),
        pltpu.HBM((64, 64, levels), F32),
        "adjoint_b",
        fields,
        g,
        in_hbm(gradient),
        specs=[vmem, vmem, hbm],
        outs=hbm,
        scratch=half,
        grant=14,
        alias={2: 0},
    )
    gradient = call(
        edge_body,
        pltpu.HBM((64, 64, levels), F32),
        "edges",
        from_left,
        from_right,
        from_above,
        from_below,
        in_hbm(gradient),
        specs=[vmem, vmem, vmem, vmem, hbm],
        outs=hbm,
        scratch=[
            pltpu.VMEM((2, 64, 8, levels), F32),
            pltpu.VMEM((2, 48, levels), F32),
            pltpu.SemaphoreType.DMA((4,)),
            pltpu.SemaphoreType.DMA((4,)),
        ],
        alias={4: 0},
    )
    return (departures, gradient)


def solution(mesh):
    return jax.shard_map(
        per_device,
        mesh=mesh,
        in_specs=(
            P(AXES, None),
            P(),
            P(AXES, None),
            P(AXES),
            P(AXES),
            P(AXES, None),
            P("lat", "lon", None),
            P(),
            P(),
            P(),
            P(),
            P(),
        ),
        out_specs=(P(AXES, None), P("lat", "lon", None)),
        check_vma=False,
    )
```

```python
import functools

import jax
import jax.numpy as jnp
from jax import lax
from jax.experimental import pallas as pl
from jax.experimental.pallas import tpu as pltpu
from jax.sharding import PartitionSpec as P

CAP = 16
F32 = jnp.float32
BF16 = jnp.bfloat16
I32 = jnp.int32
NT = (((1,), (1,)), ((), ()))
AXES = ("lat", "lon")


def iota(shape, dim):
    return lax.broadcasted_iota(I32, shape, dim)


def mm(a, b):
    return jnp.dot(a, b, preferred_element_type=F32)


def ones_where(mask):
    return jnp.where(mask, 1.0, 0.0).astype(BF16)


def call(body, out_shape, *args, scratch=(), specs=None, outs=None, grant=8, alias=None):
    vmem = pl.BlockSpec(memory_space=pltpu.VMEM)
    return pl.pallas_call(
        body,
        in_specs=specs or [vmem] * len(args),
        out_specs=outs or jax.tree.map(lambda s: vmem, out_shape),
        out_shape=out_shape,
        scratch_shapes=scratch,
        input_output_aliases=alias or {},
        compiler_params=pltpu.CompilerParams(vmem_limit_bytes=grant << 20) if grant else None,
    )(*args)


def route_body(dest_ref, row_ref, col_ref, weight_ref, send_ref, place_ref):
    dest = dest_ref[...]
    tiles = send_ref.shape[0]
    obs = dest.shape[1]
    onehot = jnp.where(iota((tiles, obs), 0) == dest, 1.0, 0.0)
    before = ones_where(iota((obs, obs), 0) < iota((obs, obs), 1))
    rank = mm(onehot.astype(BF16), before)
    slot = jnp.sum(onehot * rank, axis=0, keepdims=True).astype(I32)
    place_ref[...] = dest * CAP + slot
    here = iota((CAP, obs), 0) == slot
    weights = weight_ref[...].astype(F32)
    fields = [weights[k : k + 1] for k in range(4)]
    fields += [row_ref[...].astype(F32), col_ref[...].astype(F32)]
    parts = [jnp.where(here, field, 0.0) for field in fields]
    parts.append(jnp.zeros((128 - CAP * len(parts), obs), F32))
    table = jnp.concatenate(parts, 0).astype(BF16)
    send_ref[...] = lax.dot_general(onehot.astype(BF16), table, NT, preferred_element_type=F32)


def border_body(state_ref, first_ref, last_ref, head_ref, tail_ref, sides, rows, sems):
    edges = [
        (state_ref.at[:, pl.ds(0, 8), :], sides.at[0]),
        (state_ref.at[:, pl.ds(56, 8), :], sides.at[1]),
        (state_ref.at[0], rows.at[0]),
        (state_ref.at[63], rows.at[1]),
    ]
    copies = [pltpu.make_async_copy(a, b, sems.at[i]) for i, (a, b) in enumerate(edges)]
    for copy in copies:
        copy.start()
    for copy in copies:
        copy.wait()
    first_ref[...] = sides[0, :, 0, :]
    last_ref[...] = sides[1, :, 7, :]
    head_ref[...] = rows[0]
    tail_ref[...] = rows[1]


def fields_by_row(recv, first, count):
    tiles = recv.shape[0]
    pick = ones_where((iota((count, tiles), 0) + first) // CAP == iota((count, tiles), 1))
    mine = mm(pick, recv)
    mine = jnp.where(iota((count, 128), 0) % CAP == iota((count, 128), 1) % CAP, mine, 0.0)
    spread = ones_where(iota((128, 768), 0) // CAP == iota((128, 768), 1) // 128)
    out = mm(mine.astype(BF16), spread)
    return [out[:, 128 * k : 128 * k + 128] for k in range(6)]


def fields_by_lane(recv, slots):
    tiles = recv.shape[0]
    pick = ones_where(iota((tiles, slots), 1) // CAP == iota((tiles, slots), 0))
    mine = mm(recv.astype(F32).T.astype(BF16), pick)
    mine = jnp.where(iota((128, slots), 1) % CAP == iota((128, slots), 0) % CAP, mine, 0.0)
    gather = ones_where(iota((8, 128), 1) // CAP == iota((8, 128), 0))
    out = mm(gather, mine.astype(BF16))
    return [out[k : k + 1] for k in range(6)]


def pair_of(hit0, value0, hit1, value1):
    return jnp.where(hit0, value0, jnp.where(hit1, value1, jnp.zeros((), value0.dtype)))


def gather_body(recv_ref, own_hbm, top_ref, bottom_ref, left_ref, right_ref, out_ref, own_ref, buffer, own_sem, out_sems, rim_ref, *matrices):
    slots = out_ref.shape[0]
    chunk = matrices[0].shape[0]
    load = pltpu.make_async_copy(own_hbm, own_ref, own_sem)
    load.start()
    rim_ref[0:64, :] = top_ref[...]
    rim_ref[64:128, :] = bottom_ref[...]
    rim_ref[128:192, :] = left_ref[0:64, :]
    rim_ref[192:256, :] = right_ref[0:64, :]
    rim_ref[256:272, :] = left_ref[64:80, :]
    rim_ref[272:288, :] = right_ref[64:80, :]
    rim_ref[288:384, :] = jnp.zeros((96, rim_ref.shape[1]), BF16)
    recv = recv_ref[...].astype(BF16)
    lane = iota((chunk, 128), 1).astype(F32)
    upper = jnp.where(lane >= 64.0, 1.0, 0.0)
    in_row = (lane - 64.0 * upper).astype(BF16)
    upper = upper.astype(BF16)
    lane = lane.astype(BF16)

    def build(first, matrix_ref):
        w0, w1, w2, w3, row, col = [f.astype(BF16) for f in fields_by_row(recv, first, chunk)]
        at0, at1 = in_row == col - 1.0, in_row == col
        p0 = pair_of(at0, w0, at1, w2)
        p1 = pair_of(at0, w1, at1, w3)
        zero = jnp.zeros((), BF16)
        edge = 65.0 * upper
        matrix_ref[:, 4096:4224] = pair_of(edge == row, p0, edge == row + 1.0, p1)
        high = upper > 0.5
        side = pair_of(in_row == row - 1.0, jnp.where(high, w2, w0), in_row == row, jnp.where(high, w3, w1))
        matrix_ref[:, 4224:4352] = jnp.where(col == 64.0 * upper, side, zero)
        corner = pair_of(lane == 0.0, w0, lane == 1.0, w1) + pair_of(lane == 16.0, w2, lane == 17.0, w3)
        at_col = jnp.where(lane < 16.0, zero, zero + 64.0)
        odd = jnp.where(lane < 16.0, lane, lane - 16.0)
        matrix_ref[:, 4352:4480] = jnp.where(row == 64.0 * odd, jnp.where(col == at_col, corner, zero), zero)
        offset = row - upper
        for j in range(32):
            matrix_ref[:, 128 * j : 128 * j + 128] = pair_of(offset == 2.0 * j + 1.0, p0, offset == 2.0 * j, p1)

    def use(first, matrix_ref):
        out = mm(matrix_ref[:, :4096], own_ref[...]) + mm(matrix_ref[:, 4096:], rim_ref[...])
        at = slice(first, first + chunk)
        buffer[at, :] = out.astype(BF16)
        copies.append(pltpu.make_async_copy(buffer.at[at, :], out_ref.at[at, :], out_sems.at[len(copies)]))
        copies[-1].start()

    copies = []
    count = slots // chunk
    build(0, matrices[0])
    load.wait()
    for i in range(count):
        if i + 1 < count:
            build((i + 1) * chunk, matrices[i + 1])
        use(i * chunk, matrices[i])
    for copy in copies:
        copy.wait()


def components_body(spectra_ref, basis_ref, place_ref, pcs_ref, buffer, basis_buffer, sems, basis_sem):
    obs = spectra_ref.shape[0]
    blocks = buffer.shape[0]
    rows = obs // blocks

    def load(i):
        at = pl.ds(pl.multiple_of(i * rows, rows), rows)
        return pltpu.make_async_copy(spectra_ref.at[at, :], buffer.at[i], sems.at[i])

    basis = pltpu.make_async_copy(basis_ref, basis_buffer, basis_sem)
    basis.start()
    load(0).start()
    load(1).start()
    basis.wait()

    def step(i, carry):
        load(i).wait()

        @pl.when(i + 2 < blocks)
        def _():
            load(i + 2).start()

        at = pl.ds(pl.multiple_of(i * rows, rows), rows)
        pcs_ref[at, :] = mm(buffer[i], basis_buffer[...]).astype(BF16)
        return carry

    lax.fori_loop(0, blocks, step, 0)


def network_body(recv_ref, place_ref, pcs_ref, inv_ref, w_in_hbm, b_in_ref, w_out_hbm, b_out_ref, dep_ref, send_ref, pack_ref, unpack_ref, w_in_ref, w_out_ref, g_ref, dep_buffer, send_buffer, w_sems, dep_sems, send_sems):
    slots = recv_ref.shape[0]
    obs = pcs_ref.shape[0]
    loads = [pltpu.make_async_copy(w_in_hbm, w_in_ref, w_sems.at[0]), pltpu.make_async_copy(w_out_hbm, w_out_ref, w_sems.at[1])]
    for copy in loads:
        copy.start()
    inv = inv_ref[...]
    copies = []
    block = obs // 4
    place = place_ref[...]
    wide = jnp.broadcast_to(place.astype(F32), (128, obs)).T
    lane = iota((block, 128), 1).astype(F32)
    for i in range(4):
        at = slice(i * block, (i + 1) * block)
        for b in range(slots // 128):
            unpack_ref[at, 128 * b : 128 * b + 128] = ones_where(wide[at] - 128.0 * b == lane)
        half = slots // 4
        pack_ref[i * half : (i + 1) * half, :] = ones_where(iota((half, obs), 0) + i * half == place)
        column = mm(unpack_ref[at, :], recv_ref[...]).astype(BF16)
        if i == 0:
            for copy in loads:
                copy.wait()
        pre = mm(column, w_in_ref[...]) + b_in_ref[...]
        sig = jax.nn.sigmoid(pre)
        hidden = (pre * sig).astype(BF16)
        sim = mm(hidden, w_out_ref[...]) + b_out_ref[...]
        dep = (sim - pcs_ref[at, :].astype(F32)) * inv
        dep_buffer[at, :] = dep.astype(BF16)
        copies.append(pltpu.make_async_copy(dep_buffer.at[at, :], dep_ref.at[at, :], dep_sems.at[i]))
        copies[-1].start()
        g_sim = (dep * inv).astype(BF16)
        g_hidden = lax.dot_general(g_sim, w_out_ref[...], NT, preferred_element_type=F32)
        g_pre = (g_hidden * sig * (1.0 + pre * (1.0 - sig))).astype(BF16)
        g_ref[at, :] = lax.dot_general(g_pre, w_in_ref[...], NT, preferred_element_type=F32).astype(BF16)
    block = slots // 4
    for i in range(4):
        at = slice(i * block, (i + 1) * block)
        send_buffer[at, :] = mm(pack_ref[at, :], g_ref[...]).astype(BF16)
        copies.append(pltpu.make_async_copy(send_buffer.at[at, :], send_ref.at[at, :], send_sems.at[i]))
        copies[-1].start()
    for copy in copies:
        copy.wait()


def prepare_body(recv_ref, fields_ref):
    fields = fields_by_lane(recv_ref[...].astype(BF16), fields_ref.shape[1])
    fields_ref[...] = jnp.concatenate(fields + [fields[5], fields[5]], 0)


def scatter_rim_body(fields_ref, g_ref, up_ref, down_ref, left_ref, right_ref, rim_ref):
    slots = g_ref.shape[0]
    w0, w1, w2, w3, row, col = [fields_ref[k : k + 1, :].astype(BF16) for k in range(6)]
    zero = jnp.zeros((), BF16)
    sub = iota((64, slots), 0).astype(F32).astype(BF16)
    at0, at1 = sub == row - 1.0, sub == row
    rim_ref[128:192, :] = jnp.where(col == 0.0, pair_of(at0, w0, at1, w1), zero)
    rim_ref[208:272, :] = jnp.where(col == 64.0, pair_of(at0, w2, at1, w3), zero)
    low = iota((16, slots), 0).astype(F32).astype(BF16)
    first, last = jnp.where(row == 0.0, zero, zero - 1.0), jnp.where(row == 64.0, zero + 1.0, zero - 1.0)
    rim_ref[192:208, :] = jnp.where(col == 0.0, pair_of(low == first, w0, low == last, w1), zero)
    rim_ref[272:288, :] = jnp.where(col == 64.0, pair_of(low == first, w2, low == last, w3), zero)
    at0, at1 = sub == col - 1.0, sub == col
    rim_ref[0:64, :] = jnp.where(row == 0.0, pair_of(at0, w0, at1, w2), zero)
    rim_ref[64:128, :] = jnp.where(row == 64.0, pair_of(at0, w1, at1, w3), zero)
    out = mm(rim_ref[...], g_ref[...])
    up_ref[...] = out[0:64]
    down_ref[...] = out[64:128]
    left_ref[...] = out[128:208].astype(BF16)
    right_ref[...] = out[208:288].astype(BF16)


def corner_body(up_ref, down_ref, left_ref, right_ref, up_out, down_out):
    at = iota((64, 128), 0)
    left = left_ref[64:80, :].astype(F32)
    right = right_ref[64:80, :].astype(F32)
    for k, (ref, out) in enumerate(((up_ref, up_out), (down_ref, down_out))):
        extra = jnp.where(at == 0, left[k : k + 1], jnp.where(at == 63, right[k : k + 1], 0.0))
        out[...] = (ref[...] + extra).astype(BF16)


def scatter_body(half, fields_ref, g_ref, *refs):
    out_ref, buffer, sems = refs[-5:-2]
    matrices = refs[-2:]
    slots = g_ref.shape[0]
    rows = 16
    w0, w1, w2, w3, row, col = [fields_ref[k : k + 1, :].astype(BF16) for k in range(6)]
    sub = iota((64, slots), 0).astype(F32).astype(BF16)
    at0, at1 = sub == col - 1.0, sub == col
    p0 = pair_of(at0, w0, at1, w2)
    p1 = pair_of(at0, w1, at1, w3)
    row = jnp.broadcast_to(row, (64, slots))

    def build(first, matrix_ref):
        for j in range(rows):
            at = float(first + j)
            matrix_ref[64 * j : 64 * j + 64, :] = pair_of(row == at + 1.0, p0, row == at, p1)

    copies = []
    build(32 * half, matrices[0])
    for i in range(2):
        first = 32 * half + rows * i
        if i == 0:
            build(first + rows, matrices[1])
        out = mm(matrices[i][...], g_ref[...])
        buffer[i] = out.reshape(rows, 64, out.shape[1])
        copies.append(pltpu.make_async_copy(buffer.at[i], out_ref.at[pl.ds(first, rows)], sems.at[i]))
        copies[i].start()
    for copy in copies:
        copy.wait()


def edge_body(left_ref, right_ref, above_ref, below_ref, grad_ref, out_ref, sides, rows, in_sems, out_sems):
    edges = [
        (out_ref.at[:, pl.ds(0, 8), :], sides.at[0]),
        (out_ref.at[:, pl.ds(56, 8), :], sides.at[1]),
        (out_ref.at[0, pl.ds(8, 48), :], rows.at[0]),
        (out_ref.at[63, pl.ds(8, 48), :], rows.at[1]),
    ]
    loads = [pltpu.make_async_copy(a, b, in_sems.at[i]) for i, (a, b) in enumerate(edges)]
    stores = [pltpu.make_async_copy(b, a, out_sems.at[i]) for i, (a, b) in enumerate(edges)]
    for copy in loads:
        copy.start()
    for copy in loads:
        copy.wait()
    above, below = above_ref[...].astype(F32), below_ref[...].astype(F32)
    sides[0, :, 0, :] += left_ref[0:64, :].astype(F32)
    sides[1, :, 7, :] += right_ref[0:64, :].astype(F32)
    sides[0, 0] += above[0:8]
    sides[1, 0] += above[56:64]
    sides[0, 63] += below[0:8]
    sides[1, 63] += below[56:64]
    rows[0] += above[8:56]
    rows[1] += below[8:56]
    for copy in stores:
        copy.start()
    for copy in stores:
        copy.wait()


def in_hbm(x):
    return pltpu.with_memory_space_constraint(x, pltpu.HBM)


def shift(x, axis, step, closed):
    count = lax.axis_size(axis)
    pairs = [(i, (i + step) % count) for i in range(count) if closed or 0 <= i + step < count]
    return lax.ppermute(x, axis, pairs)


def exchange(x):
    return lax.all_to_all(x, AXES, split_axis=0, concat_axis=0, tiled=True)


def per_device(
    spectra,
    pc_basis,
    destination,
    corner_row,
    corner_col,
    corner_weight,
    state,
    inv_sigma,
    w_in,
    b_in,
    w_out,
    b_out,
):
    tiles = lax.axis_size("lat") * lax.axis_size("lon")
    obs = spectra.shape[0]
    npc = pc_basis.shape[1]
    levels = state.shape[2]
    slots = tiles * CAP
    sds = jax.ShapeDtypeStruct

    vmem = pl.BlockSpec(memory_space=pltpu.VMEM)
    hbm = pl.BlockSpec(memory_space=pltpu.HBM)
    send_meta, place = call(
        route_body,
        (pltpu.HBM((tiles, 128), F32), sds((1, obs), I32)),
        destination.reshape(1, obs),
        corner_row.reshape(1, obs),
        corner_col.reshape(1, obs),
        corner_weight.T,
        grant=None,
    )
    recv_meta = exchange(send_meta)
    first, last, head, tail = call(
        border_body,
        (sds((64, levels), BF16),) * 4,
        in_hbm(state),
        specs=[hbm],
        scratch=[
            pltpu.VMEM((2, 64, 8, levels), BF16),
            pltpu.VMEM((2, 64, levels), BF16),
            pltpu.SemaphoreType.DMA((4,)),
        ],
    )
    top = shift(tail, "lat", 1, False)
    bottom = shift(head, "lat", -1, False)
    fill = jnp.zeros((14, levels), BF16)
    left = shift(jnp.concatenate([last, top[63:], bottom[63:], fill], 0), "lon", 1, True)
    right = shift(jnp.concatenate([first, top[:1], bottom[:1], fill], 0), "lon", -1, True)

    columns = call(
        gather_body,
        pltpu.HBM((slots, levels), BF16),
        recv_meta,
        in_hbm(state.reshape(-1, levels)),
        top,
        bottom,
        left,
        right,
        specs=[vmem, hbm, vmem, vmem, vmem, vmem],
        outs=hbm,
        scratch=[
            pltpu.VMEM((4096, levels), BF16),
            pltpu.VMEM((slots, levels), BF16),
            pltpu.SemaphoreType.DMA,
            pltpu.SemaphoreType.DMA((4,)),
            pltpu.VMEM((384, levels), BF16),
        ]
        + [pltpu.VMEM((slots // 4, 4480), BF16)] * 4,
        grant=28,
    )
    columns, place = lax.optimization_barrier((columns, place))
    recv_columns = exchange(columns.reshape(tiles, CAP, levels)).reshape(slots, levels)
    pcs = call(
        components_body,
        sds((obs, npc), BF16),
        in_hbm(spectra),
        in_hbm(pc_basis),
        place,
        specs=[hbm, hbm, vmem],
        scratch=[
            pltpu.VMEM((4, obs // 4, spectra.shape[1]), BF16),
            pltpu.VMEM(pc_basis.shape, BF16),
            pltpu.SemaphoreType.DMA((4,)),
            pltpu.SemaphoreType.DMA,
        ],
        grant=26,
    )
    departures, send_g = call(
        network_body,
        (pltpu.HBM((obs, npc), BF16), pltpu.HBM((slots, levels), BF16)),
        recv_columns,
        place,
        pcs,
        inv_sigma[None],
        in_hbm(w_in),
        b_in[None],
        in_hbm(w_out),
        b_out[None],
        specs=[vmem] * 4 + [hbm, vmem, hbm, vmem],
        outs=(hbm, hbm),
        scratch=[
            pltpu.VMEM((slots, obs), BF16),
            pltpu.VMEM((obs, slots), BF16),
            pltpu.VMEM(w_in.shape, BF16),
            pltpu.VMEM(w_out.shape, BF16),
            pltpu.VMEM((obs, levels), BF16),
            pltpu.VMEM((obs, npc), BF16),
            pltpu.VMEM((slots, levels), BF16),
            pltpu.SemaphoreType.DMA((2,)),
            pltpu.SemaphoreType.DMA((4,)),
            pltpu.SemaphoreType.DMA((4,)),
        ],
        grant=24,
    )
    send_g, recv_meta = lax.optimization_barrier((send_g, recv_meta))
    g = exchange(send_g.reshape(tiles, CAP, levels)).reshape(slots, levels)
    fields = call(prepare_body, sds((8, slots), F32), recv_meta)
    up, down, g_left, g_right = call(
        scatter_rim_body,
        (sds((64, levels), F32), sds((64, levels), F32), sds((80, levels), BF16), sds((80, levels), BF16)),
        fields,
        g,
        scratch=[pltpu.VMEM((288, slots), BF16)],
    )
    from_right = shift(g_left, "lon", -1, True)
    from_left = shift(g_right, "lon", 1, True)
    half = [pltpu.VMEM((2, 16, 64, levels), F32), pltpu.SemaphoreType.DMA((2,))]
    half += [pltpu.VMEM((1024, slots), BF16)] * 2
    gradient = call(
        functools.partial(scatter_body, 0),
        pltpu.HBM((64, 64, levels), F32),
        fields,
        g,
        outs=hbm,
        scratch=half,
        grant=14,
    )
    from_left, from_right, gradient = lax.optimization_barrier((from_left, from_right, gradient))
    up, down = call(corner_body, (sds((64, levels), BF16), sds((64, levels), BF16)), up, down, from_left, from_right)
    up, down, g = lax.optimization_barrier((up, down, g))
    from_below = shift(up, "lat", -1, False)
    from_above = shift(down, "lat", 1, False)
    gradient = call(
        functools.partial(scatter_body, 1),
        pltpu.HBM((64, 64, levels), F32),
        fields,
        g,
        in_hbm(gradient),
        specs=[vmem, vmem, hbm],
        outs=hbm,
        scratch=half,
        grant=14,
        alias={2: 0},
    )
    gradient = call(
        edge_body,
        pltpu.HBM((64, 64, levels), F32),
        from_left,
        from_right,
        from_above,
        from_below,
        in_hbm(gradient),
        specs=[vmem, vmem, vmem, vmem, hbm],
        outs=hbm,
        scratch=[
            pltpu.VMEM((2, 64, 8, levels), F32),
            pltpu.VMEM((2, 48, levels), F32),
            pltpu.SemaphoreType.DMA((4,)),
            pltpu.SemaphoreType.DMA((4,)),
        ],
        alias={4: 0},
    )
    return (departures, gradient)


def solution(mesh):
    return jax.shard_map(
        per_device,
        mesh=mesh,
        in_specs=(
            P(AXES, None),
            P(),
            P(AXES, None),
            P(AXES),
            P(AXES),
            P(AXES, None),
            P("lat", "lon", None),
            P(),
            P(),
            P(),
            P(),
            P(),
        ),
        out_specs=(P(AXES, None), P("lat", "lon", None)),
        check_vma=False,
    )
```

```python
import functools

import jax
import jax.numpy as jnp
from jax import lax
from jax.experimental import pallas as pl
from jax.experimental.pallas import tpu as pltpu
from jax.sharding import PartitionSpec as P

CAP = 16
F32 = jnp.float32
BF16 = jnp.bfloat16
I32 = jnp.int32
NT = (((1,), (1,)), ((), ()))
AXES = ("lat", "lon")


def iota(shape, dim):
    return lax.broadcasted_iota(I32, shape, dim)


def mm(a, b):
    return jnp.dot(a, b, preferred_element_type=F32)


def ones_where(mask):
    return jnp.where(mask, 1.0, 0.0).astype(BF16)


def call(body, out_shape, *args, scratch=(), specs=None, outs=None, grant=8, alias=None):
    vmem = pl.BlockSpec(memory_space=pltpu.VMEM)
    return pl.pallas_call(
        body,
        in_specs=specs or [vmem] * len(args),
        out_specs=outs or jax.tree.map(lambda s: vmem, out_shape),
        out_shape=out_shape,
        scratch_shapes=scratch,
        input_output_aliases=alias or {},
        compiler_params=pltpu.CompilerParams(vmem_limit_bytes=grant << 20) if grant else None,
    )(*args)


def diagonal(rows, cols):
    lat, lon, n_lat, n_lon = lax.axis_index("lat"), lax.axis_index("lon"), lax.axis_size("lat"), lax.axis_size("lon")
    to = lat + rows
    return jnp.where((to >= 0) & (to < n_lat), to * n_lon + (lon + cols + n_lon) % n_lon, -1)


def route_body(dest_ref, row_ref, col_ref, weight_ref, state_ref, send_ref, place_ref, cells, sems):
    spots = [(0, 0), (0, 56), (63, 0), (63, 56)]
    copies = [
        pltpu.make_async_copy(state_ref.at[r, pl.ds(c, 8), :], cells.at[i], sems.at[i]) for i, (r, c) in enumerate(spots)
    ]
    for copy in copies:
        copy.start()
    dest = dest_ref[...]
    tiles = send_ref.shape[0] // 2
    obs = dest.shape[1]
    onehot = jnp.where(iota((tiles, obs), 0) == dest, 1.0, 0.0)
    before = ones_where(iota((obs, obs), 0) < iota((obs, obs), 1))
    rank = mm(onehot.astype(BF16), before)
    slot = jnp.sum(onehot * rank, axis=0, keepdims=True).astype(I32)
    place_ref[...] = dest * CAP + slot
    here = iota((CAP, obs), 0) == slot
    weights = weight_ref[...].astype(F32)
    fields = [weights[k : k + 1] for k in range(4)]
    fields += [row_ref[...].astype(F32), col_ref[...].astype(F32)]
    parts = [jnp.where(here, field, 0.0) for field in fields]
    parts.append(jnp.zeros((128 - CAP * len(parts), obs), F32))
    table = jnp.concatenate(parts, 0).astype(BF16)
    send_ref[pl.ds(0, tiles, stride=2), :] = lax.dot_general(
        onehot.astype(BF16), table, NT, preferred_element_type=F32
    )
    for copy in copies:
        copy.wait()
    row = iota((tiles, 128), 0)
    extra = jnp.zeros((tiles, 128), F32)
    for i, (r, c) in enumerate(spots):
        cell = cells[i].astype(F32)[7 if c else 0][None]
        extra = jnp.where(row == diagonal(1 if r else -1, 1 if c else -1), cell, extra)
    send_ref[pl.ds(1, tiles, stride=2), :] = extra


def border_body(state_ref, first_ref, last_ref, head_ref, tail_ref, sides, rows, sems):
    edges = [
        (state_ref.at[:, pl.ds(0, 8), :], sides.at[0]),
        (state_ref.at[:, pl.ds(56, 8), :], sides.at[1]),
        (state_ref.at[0], rows.at[0]),
        (state_ref.at[63], rows.at[1]),
    ]
    copies = [pltpu.make_async_copy(a, b, sems.at[i]) for i, (a, b) in enumerate(edges)]
    for copy in copies:
        copy.start()
    for copy in copies:
        copy.wait()
    first_ref[...] = sides[0, :, 0, :]
    last_ref[...] = sides[1, :, 7, :]
    head_ref[...] = rows[0]
    tail_ref[...] = rows[1]


def fields_by_row(recv, first, count):
    tiles = recv.shape[0]
    pick = ones_where((iota((count, tiles), 0) + first) // CAP == iota((count, tiles), 1))
    mine = mm(pick, recv)
    mine = jnp.where(iota((count, 128), 0) % CAP == iota((count, 128), 1) % CAP, mine, 0.0)
    spread = ones_where(iota((128, 768), 0) // CAP == iota((128, 768), 1) // 128)
    out = mm(mine.astype(BF16), spread)
    return [out[:, 128 * k : 128 * k + 128] for k in range(6)]


def fields_by_lane(recv, slots):
    tiles = recv.shape[0]
    pick = ones_where(iota((tiles, slots), 1) // CAP == iota((tiles, slots), 0))
    mine = mm(recv.astype(F32).T.astype(BF16), pick)
    mine = jnp.where(iota((128, slots), 1) % CAP == iota((128, slots), 0) % CAP, mine, 0.0)
    gather = ones_where(iota((8, 128), 1) // CAP == iota((8, 128), 0))
    out = mm(gather, mine.astype(BF16))
    return [out[k : k + 1] for k in range(6)]


def pair_of(hit0, value0, hit1, value1):
    return jnp.where(hit0, value0, jnp.where(hit1, value1, jnp.zeros((), value0.dtype)))


def gather_body(recv_ref, own_hbm, top_ref, bottom_ref, left_ref, right_ref, out_ref, own_ref, buffer, own_sem, out_sems, rim_ref, *matrices):
    slots = out_ref.shape[0]
    chunk = matrices[0].shape[0]
    load = pltpu.make_async_copy(own_hbm, own_ref, own_sem)
    load.start()
    rim_ref[0:64, :] = top_ref[...]
    rim_ref[64:128, :] = bottom_ref[...]
    rim_ref[128:192, :] = left_ref[...]
    rim_ref[192:256, :] = right_ref[...]
    tiles = recv_ref.shape[0] // 2
    cells = recv_ref[pl.ds(1, tiles, stride=2), :].astype(BF16)
    row, lane = iota((16, tiles), 0), iota((16, tiles), 1)
    for i, side in enumerate((-1, 1)):
        source = jnp.where(row == 0, diagonal(-1, side), jnp.where(row == 1, diagonal(1, side), -1))
        rim_ref[256 + 16 * i : 272 + 16 * i, :] = mm(ones_where(lane == source), cells).astype(BF16)
    rim_ref[288:384, :] = jnp.zeros((96, rim_ref.shape[1]), BF16)
    recv = recv_ref[pl.ds(0, tiles, stride=2), :].astype(BF16)
    lane = iota((chunk, 128), 1).astype(F32)
    upper = jnp.where(lane >= 64.0, 1.0, 0.0)
    in_row = (lane - 64.0 * upper).astype(BF16)
    upper = upper.astype(BF16)
    lane = lane.astype(BF16)

    def build(first, matrix_ref):
        w0, w1, w2, w3, row, col = [f.astype(BF16) for f in fields_by_row(recv, first, chunk)]
        at0, at1 = in_row == col - 1.0, in_row == col
        p0 = pair_of(at0, w0, at1, w2)
        p1 = pair_of(at0, w1, at1, w3)
        zero = jnp.zeros((), BF16)
        edge = 65.0 * upper
        matrix_ref[:, 4096:4224] = pair_of(edge == row, p0, edge == row + 1.0, p1)
        high = upper > 0.5
        side = pair_of(in_row == row - 1.0, jnp.where(high, w2, w0), in_row == row, jnp.where(high, w3, w1))
        matrix_ref[:, 4224:4352] = jnp.where(col == 64.0 * upper, side, zero)
        corner = pair_of(lane == 0.0, w0, lane == 1.0, w1) + pair_of(lane == 16.0, w2, lane == 17.0, w3)
        at_col = jnp.where(lane < 16.0, zero, zero + 64.0)
        odd = jnp.where(lane < 16.0, lane, lane - 16.0)
        matrix_ref[:, 4352:4480] = jnp.where(row == 64.0 * odd, jnp.where(col == at_col, corner, zero), zero)
        offset = row - upper
        for j in range(32):
            matrix_ref[:, 128 * j : 128 * j + 128] = pair_of(offset == 2.0 * j + 1.0, p0, offset == 2.0 * j, p1)

    def use(first, matrix_ref):
        out = mm(matrix_ref[:, :4096], own_ref[...]) + mm(matrix_ref[:, 4096:], rim_ref[...])
        at = slice(first, first + chunk)
        buffer[at, :] = out.astype(BF16)
        copies.append(pltpu.make_async_copy(buffer.at[at, :], out_ref.at[at, :], out_sems.at[len(copies)]))
        copies[-1].start()

    copies = []
    count = slots // chunk
    build(0, matrices[0])
    load.wait()
    for i in range(count):
        if i + 1 < count:
            build((i + 1) * chunk, matrices[i + 1])
        use(i * chunk, matrices[i])
    for copy in copies:
        copy.wait()


def components_body(spectra_ref, basis_ref, place_ref, pcs_ref, buffer, basis_buffer, sems, basis_sem):
    obs = spectra_ref.shape[0]
    blocks = buffer.shape[0]
    rows = obs // blocks

    def load(i):
        at = pl.ds(pl.multiple_of(i * rows, rows), rows)
        return pltpu.make_async_copy(spectra_ref.at[at, :], buffer.at[i], sems.at[i])

    basis = pltpu.make_async_copy(basis_ref, basis_buffer, basis_sem)
    basis.start()
    load(0).start()
    load(1).start()
    basis.wait()

    def step(i, carry):
        load(i).wait()

        @pl.when(i + 2 < blocks)
        def _():
            load(i + 2).start()

        at = pl.ds(pl.multiple_of(i * rows, rows), rows)
        pcs_ref[at, :] = mm(buffer[i], basis_buffer[...]).astype(BF16)
        return carry

    lax.fori_loop(0, blocks, step, 0)


def network_body(recv_ref, place_ref, pcs_ref, inv_ref, w_in_hbm, b_in_ref, w_out_hbm, b_out_ref, dep_ref, send_ref, pack_ref, unpack_ref, w_in_ref, w_out_ref, g_ref, dep_buffer, send_buffer, w_sems, dep_sems, send_sems):
    slots = recv_ref.shape[0]
    obs = pcs_ref.shape[0]
    loads = [pltpu.make_async_copy(w_in_hbm, w_in_ref, w_sems.at[0]), pltpu.make_async_copy(w_out_hbm, w_out_ref, w_sems.at[1])]
    for copy in loads:
        copy.start()
    inv = inv_ref[...]
    copies = []
    block = obs // 4
    place = place_ref[...]
    wide = jnp.broadcast_to(place.astype(F32), (128, obs)).T
    lane = iota((block, 128), 1).astype(F32)
    for i in range(4):
        at = slice(i * block, (i + 1) * block)
        for b in range(slots // 128):
            unpack_ref[at, 128 * b : 128 * b + 128] = ones_where(wide[at] - 128.0 * b == lane)
        half = slots // 4
        pack_ref[i * half : (i + 1) * half, :] = ones_where(iota((half, obs), 0) + i * half == place)
        column = mm(unpack_ref[at, :], recv_ref[...]).astype(BF16)
        if i == 0:
            for copy in loads:
                copy.wait()
        pre = mm(column, w_in_ref[...]) + b_in_ref[...]
        sig = jax.nn.sigmoid(pre)
        hidden = (pre * sig).astype(BF16)
        sim = mm(hidden, w_out_ref[...]) + b_out_ref[...]
        dep = (sim - pcs_ref[at, :].astype(F32)) * inv
        dep_buffer[at, :] = dep.astype(BF16)
        copies.append(pltpu.make_async_copy(dep_buffer.at[at, :], dep_ref.at[at, :], dep_sems.at[i]))
        copies[-1].start()
        g_sim = (dep * inv).astype(BF16)
        g_hidden = lax.dot_general(g_sim, w_out_ref[...], NT, preferred_element_type=F32)
        g_pre = (g_hidden * sig * (1.0 + pre * (1.0 - sig))).astype(BF16)
        g_ref[at, :] = lax.dot_general(g_pre, w_in_ref[...], NT, preferred_element_type=F32).astype(BF16)
    block = slots // 4
    for i in range(4):
        at = slice(i * block, (i + 1) * block)
        send_buffer[at, :] = mm(pack_ref[at, :], g_ref[...]).astype(BF16)
        copies.append(pltpu.make_async_copy(send_buffer.at[at, :], send_ref.at[at, :], send_sems.at[i]))
        copies[-1].start()
    for copy in copies:
        copy.wait()


def prepare_body(recv_ref, fields_ref):
    fields = fields_by_lane(recv_ref[pl.ds(0, recv_ref.shape[0] // 2, stride=2), :].astype(BF16), fields_ref.shape[1])
    fields_ref[...] = jnp.concatenate(fields + [fields[5], fields[5]], 0)


def scatter_rim_body(fields_ref, g_ref, up_ref, down_ref, left_ref, right_ref, rim_ref):
    slots = g_ref.shape[0]
    w0, w1, w2, w3, row, col = [fields_ref[k : k + 1, :].astype(BF16) for k in range(6)]
    zero = jnp.zeros((), BF16)
    sub = iota((64, slots), 0).astype(F32).astype(BF16)
    at0, at1 = sub == row - 1.0, sub == row
    rim_ref[128:192, :] = jnp.where(col == 0.0, pair_of(at0, w0, at1, w1), zero)
    rim_ref[208:272, :] = jnp.where(col == 64.0, pair_of(at0, w2, at1, w3), zero)
    low = iota((16, slots), 0).astype(F32).astype(BF16)
    first, last = jnp.where(row == 0.0, zero, zero - 1.0), jnp.where(row == 64.0, zero + 1.0, zero - 1.0)
    rim_ref[192:208, :] = jnp.where(col == 0.0, pair_of(low == first, w0, low == last, w1), zero)
    rim_ref[272:288, :] = jnp.where(col == 64.0, pair_of(low == first, w2, low == last, w3), zero)
    at0, at1 = sub == col - 1.0, sub == col
    rim_ref[0:64, :] = jnp.where(row == 0.0, pair_of(at0, w0, at1, w2), zero)
    rim_ref[64:128, :] = jnp.where(row == 64.0, pair_of(at0, w1, at1, w3), zero)
    out = mm(rim_ref[...], g_ref[...])
    up_ref[...] = out[0:64]
    down_ref[...] = out[64:128]
    left_ref[...] = out[128:208].astype(BF16)
    right_ref[...] = out[208:288].astype(BF16)


def corner_body(up_ref, down_ref, left_ref, right_ref, up_out, down_out):
    at = iota((64, 128), 0)
    left = left_ref[64:80, :].astype(F32)
    right = right_ref[64:80, :].astype(F32)
    for k, (ref, out) in enumerate(((up_ref, up_out), (down_ref, down_out))):
        extra = jnp.where(at == 0, left[k : k + 1], jnp.where(at == 63, right[k : k + 1], 0.0))
        out[...] = (ref[...] + extra).astype(BF16)


def scatter_body(half, fields_ref, g_ref, *refs):
    out_ref, buffer, sems = refs[-5:-2]
    matrices = refs[-2:]
    slots = g_ref.shape[0]
    rows = 16
    w0, w1, w2, w3, row, col = [fields_ref[k : k + 1, :].astype(BF16) for k in range(6)]
    sub = iota((64, slots), 0).astype(F32).astype(BF16)
    at0, at1 = sub == col - 1.0, sub == col
    p0 = pair_of(at0, w0, at1, w2)
    p1 = pair_of(at0, w1, at1, w3)
    row = jnp.broadcast_to(row, (64, slots))

    def build(first, matrix_ref):
        for j in range(rows):
            at = float(first + j)
            matrix_ref[64 * j : 64 * j + 64, :] = pair_of(row == at + 1.0, p0, row == at, p1)

    copies = []
    build(32 * half, matrices[0])
    for i in range(2):
        first = 32 * half + rows * i
        if i == 0:
            build(first + rows, matrices[1])
        out = mm(matrices[i][...], g_ref[...])
        buffer[i] = out.reshape(rows, 64, out.shape[1])
        copies.append(pltpu.make_async_copy(buffer.at[i], out_ref.at[pl.ds(first, rows)], sems.at[i]))
        copies[i].start()
    for copy in copies:
        copy.wait()


def edge_body(left_ref, right_ref, above_ref, below_ref, grad_ref, out_ref, sides, rows, in_sems, out_sems):
    edges = [
        (out_ref.at[:, pl.ds(0, 8), :], sides.at[0]),
        (out_ref.at[:, pl.ds(56, 8), :], sides.at[1]),
        (out_ref.at[0, pl.ds(8, 48), :], rows.at[0]),
        (out_ref.at[63, pl.ds(8, 48), :], rows.at[1]),
    ]
    loads = [pltpu.make_async_copy(a, b, in_sems.at[i]) for i, (a, b) in enumerate(edges)]
    stores = [pltpu.make_async_copy(b, a, out_sems.at[i]) for i, (a, b) in enumerate(edges)]
    for copy in loads:
        copy.start()
    for copy in loads:
        copy.wait()
    above, below = above_ref[...].astype(F32), below_ref[...].astype(F32)
    sides[0, :, 0, :] += left_ref[0:64, :].astype(F32)
    sides[1, :, 7, :] += right_ref[0:64, :].astype(F32)
    sides[0, 0] += above[0:8]
    sides[1, 0] += above[56:64]
    sides[0, 63] += below[0:8]
    sides[1, 63] += below[56:64]
    rows[0] += above[8:56]
    rows[1] += below[8:56]
    for copy in stores:
        copy.start()
    for copy in stores:
        copy.wait()


def in_hbm(x):
    return pltpu.with_memory_space_constraint(x, pltpu.HBM)


def shift(x, axis, step, closed):
    count = lax.axis_size(axis)
    pairs = [(i, (i + step) % count) for i in range(count) if closed or 0 <= i + step < count]
    return lax.ppermute(x, axis, pairs)


def exchange(x):
    return lax.all_to_all(x, AXES, split_axis=0, concat_axis=0, tiled=True)


def per_device(
    spectra,
    pc_basis,
    destination,
    corner_row,
    corner_col,
    corner_weight,
    state,
    inv_sigma,
    w_in,
    b_in,
    w_out,
    b_out,
):
    tiles = lax.axis_size("lat") * lax.axis_size("lon")
    obs = spectra.shape[0]
    npc = pc_basis.shape[1]
    levels = state.shape[2]
    slots = tiles * CAP
    sds = jax.ShapeDtypeStruct

    vmem = pl.BlockSpec(memory_space=pltpu.VMEM)
    hbm = pl.BlockSpec(memory_space=pltpu.HBM)
    send_meta, place = call(
        route_body,
        (pltpu.HBM((2 * tiles, 128), F32), sds((1, obs), I32)),
        destination.reshape(1, obs),
        corner_row.reshape(1, obs),
        corner_col.reshape(1, obs),
        corner_weight.T,
        in_hbm(state),
        specs=[vmem] * 4 + [hbm],
        scratch=[pltpu.VMEM((4, 8, levels), BF16), pltpu.SemaphoreType.DMA((4,))],
        grant=None,
    )
    recv_meta = exchange(send_meta.reshape(tiles, 2, 128)).reshape(2 * tiles, 128)
    first, last, head, tail = call(
        border_body,
        (sds((64, levels), BF16),) * 4,
        in_hbm(state),
        specs=[hbm],
        scratch=[
            pltpu.VMEM((2, 64, 8, levels), BF16),
            pltpu.VMEM((2, 64, levels), BF16),
            pltpu.SemaphoreType.DMA((4,)),
        ],
    )
    top = shift(tail, "lat", 1, False)
    bottom = shift(head, "lat", -1, False)
    left = shift(last, "lon", 1, True)
    right = shift(first, "lon", -1, True)

    columns = call(
        gather_body,
        pltpu.HBM((slots, levels), BF16),
        recv_meta,
        in_hbm(state.reshape(-1, levels)),
        top,
        bottom,
        left,
        right,
        specs=[vmem, hbm, vmem, vmem, vmem, vmem],
        outs=hbm,
        scratch=[
            pltpu.VMEM((4096, levels), BF16),
            pltpu.VMEM((slots, levels), BF16),
            pltpu.SemaphoreType.DMA,
            pltpu.SemaphoreType.DMA((4,)),
            pltpu.VMEM((384, levels), BF16),
        ]
        + [pltpu.VMEM((slots // 4, 4480), BF16)] * 4,
        grant=28,
    )
    columns, place = lax.optimization_barrier((columns, place))
    recv_columns = exchange(columns.reshape(tiles, CAP, levels)).reshape(slots, levels)
    pcs = call(
        components_body,
        sds((obs, npc), BF16),
        in_hbm(spectra),
        in_hbm(pc_basis),
        place,
        specs=[hbm, hbm, vmem],
        scratch=[
            pltpu.VMEM((4, obs // 4, spectra.shape[1]), BF16),
            pltpu.VMEM(pc_basis.shape, BF16),
            pltpu.SemaphoreType.DMA((4,)),
            pltpu.SemaphoreType.DMA,
        ],
        grant=26,
    )
    departures, send_g = call(
        network_body,
        (pltpu.HBM((obs, npc), BF16), pltpu.HBM((slots, levels), BF16)),
        recv_columns,
        place,
        pcs,
        inv_sigma[None],
        in_hbm(w_in),
        b_in[None],
        in_hbm(w_out),
        b_out[None],
        specs=[vmem] * 4 + [hbm, vmem, hbm, vmem],
        outs=(hbm, hbm),
        scratch=[
            pltpu.VMEM((slots, obs), BF16),
            pltpu.VMEM((obs, slots), BF16),
            pltpu.VMEM(w_in.shape, BF16),
            pltpu.VMEM(w_out.shape, BF16),
            pltpu.VMEM((obs, levels), BF16),
            pltpu.VMEM((obs, npc), BF16),
            pltpu.VMEM((slots, levels), BF16),
            pltpu.SemaphoreType.DMA((2,)),
            pltpu.SemaphoreType.DMA((4,)),
            pltpu.SemaphoreType.DMA((4,)),
        ],
        grant=24,
    )
    send_g, recv_meta = lax.optimization_barrier((send_g, recv_meta))
    g = exchange(send_g.reshape(tiles, CAP, levels)).reshape(slots, levels)
    fields = call(prepare_body, sds((8, slots), F32), recv_meta)
    up, down, g_left, g_right = call(
        scatter_rim_body,
        (sds((64, levels), F32), sds((64, levels), F32), sds((80, levels), BF16), sds((80, levels), BF16)),
        fields,
        g,
        scratch=[pltpu.VMEM((288, slots), BF16)],
    )
    from_right = shift(g_left, "lon", -1, True)
    from_left = shift(g_right, "lon", 1, True)
    half = [pltpu.VMEM((2, 16, 64, levels), F32), pltpu.SemaphoreType.DMA((2,))]
    half += [pltpu.VMEM((1024, slots), BF16)] * 2
    gradient = call(
        functools.partial(scatter_body, 0),
        pltpu.HBM((64, 64, levels), F32),
        fields,
        g,
        outs=hbm,
        scratch=half,
        grant=14,
    )
    from_left, from_right, gradient = lax.optimization_barrier((from_left, from_right, gradient))
    up, down = call(corner_body, (sds((64, levels), BF16), sds((64, levels), BF16)), up, down, from_left, from_right)
    up, down, g = lax.optimization_barrier((up, down, g))
    from_below = shift(up, "lat", -1, False)
    from_above = shift(down, "lat", 1, False)
    gradient = call(
        functools.partial(scatter_body, 1),
        pltpu.HBM((64, 64, levels), F32),
        fields,
        g,
        in_hbm(gradient),
        specs=[vmem, vmem, hbm],
        outs=hbm,
        scratch=half,
        grant=14,
        alias={2: 0},
    )
    gradient = call(
        edge_body,
        pltpu.HBM((64, 64, levels), F32),
        from_left,
        from_right,
        from_above,
        from_below,
        in_hbm(gradient),
        specs=[vmem, vmem, vmem, vmem, hbm],
        outs=hbm,
        scratch=[
            pltpu.VMEM((2, 64, 8, levels), F32),
            pltpu.VMEM((2, 48, levels), F32),
            pltpu.SemaphoreType.DMA((4,)),
            pltpu.SemaphoreType.DMA((4,)),
        ],
        alias={4: 0},
    )
    return (departures, gradient)


def solution(mesh):
    return jax.shard_map(
        per_device,
        mesh=mesh,
        in_specs=(
            P(AXES, None),
            P(),
            P(AXES, None),
            P(AXES),
            P(AXES),
            P(AXES, None),
            P("lat", "lon", None),
            P(),
            P(),
            P(),
            P(),
            P(),
        ),
        out_specs=(P(AXES, None), P("lat", "lon", None)),
        check_vma=False,
    )
```

```python
import functools

import jax
import jax.numpy as jnp
from jax import lax
from jax.experimental import pallas as pl
from jax.experimental.pallas import tpu as pltpu
from jax.sharding import PartitionSpec as P

CAP = 16
F32 = jnp.float32
BF16 = jnp.bfloat16
I32 = jnp.int32
NT = (((1,), (1,)), ((), ()))
AXES = ("lat", "lon")


def iota(shape, dim):
    return lax.broadcasted_iota(I32, shape, dim)


def mm(a, b):
    return jnp.dot(a, b, preferred_element_type=F32)


def ones_where(mask):
    return jnp.where(mask, 1.0, 0.0).astype(BF16)


def call(body, out_shape, *args, scratch=(), specs=None, outs=None, grant=8, alias=None):
    vmem = pl.BlockSpec(memory_space=pltpu.VMEM)
    return pl.pallas_call(
        body,
        in_specs=specs or [vmem] * len(args),
        out_specs=outs or jax.tree.map(lambda s: vmem, out_shape),
        out_shape=out_shape,
        scratch_shapes=scratch,
        input_output_aliases=alias or {},
        compiler_params=pltpu.CompilerParams(vmem_limit_bytes=grant << 20) if grant else None,
    )(*args)


def diagonal(rows, cols):
    lat, lon, n_lat, n_lon = lax.axis_index("lat"), lax.axis_index("lon"), lax.axis_size("lat"), lax.axis_size("lon")
    to = lat + rows
    return jnp.where((to >= 0) & (to < n_lat), to * n_lon + (lon + cols + n_lon) % n_lon, -1)


def route_body(dest_ref, row_ref, col_ref, weight_ref, state_ref, send_ref, place_ref, first_ref, last_ref, head_ref, tail_ref, sides, rows, sems):
    edges = [
        (state_ref.at[:, pl.ds(0, 8), :], sides.at[0]),
        (state_ref.at[:, pl.ds(56, 8), :], sides.at[1]),
        (state_ref.at[0], rows.at[0]),
        (state_ref.at[63], rows.at[1]),
    ]
    copies = [pltpu.make_async_copy(a, b, sems.at[i]) for i, (a, b) in enumerate(edges)]
    for copy in copies:
        copy.start()
    dest = dest_ref[...]
    tiles = send_ref.shape[0] // 2
    obs = dest.shape[1]
    onehot = jnp.where(iota((tiles, obs), 0) == dest, 1.0, 0.0)
    before = ones_where(iota((obs, obs), 0) < iota((obs, obs), 1))
    rank = mm(onehot.astype(BF16), before)
    slot = jnp.sum(onehot * rank, axis=0, keepdims=True).astype(I32)
    place_ref[...] = dest * CAP + slot
    here = iota((CAP, obs), 0) == slot
    weights = weight_ref[...].astype(F32)
    fields = [weights[k : k + 1] for k in range(4)]
    fields += [row_ref[...].astype(F32), col_ref[...].astype(F32)]
    parts = [jnp.where(here, field, 0.0) for field in fields]
    parts.append(jnp.zeros((128 - CAP * len(parts), obs), F32))
    table = jnp.concatenate(parts, 0).astype(BF16)
    send_ref[pl.ds(0, tiles, stride=2), :] = lax.dot_general(
        onehot.astype(BF16), table, NT, preferred_element_type=F32
    )
    for copy in copies:
        copy.wait()
    first_ref[...] = sides[0, :, 0, :]
    last_ref[...] = sides[1, :, 7, :]
    head_ref[...] = rows[0]
    tail_ref[...] = rows[1]
    row = iota((tiles, 128), 0)
    extra = jnp.zeros((tiles, 128), F32)
    for r in range(2):
        for c in range(2):
            cell = sides[c, 63 * r].astype(F32)[7 * c][None]
            extra = jnp.where(row == diagonal(2 * r - 1, 2 * c - 1), cell, extra)
    send_ref[pl.ds(1, tiles, stride=2), :] = extra


def fields_by_row(recv, first, count):
    tiles = recv.shape[0]
    pick = ones_where((iota((count, tiles), 0) + first) // CAP == iota((count, tiles), 1))
    mine = mm(pick, recv)
    mine = jnp.where(iota((count, 128), 0) % CAP == iota((count, 128), 1) % CAP, mine, 0.0)
    spread = ones_where(iota((128, 768), 0) // CAP == iota((128, 768), 1) // 128)
    out = mm(mine.astype(BF16), spread)
    return [out[:, 128 * k : 128 * k + 128] for k in range(6)]


def fields_by_lane(recv, slots):
    tiles = recv.shape[0]
    pick = ones_where(iota((tiles, slots), 1) // CAP == iota((tiles, slots), 0))
    mine = mm(recv.astype(F32).T.astype(BF16), pick)
    mine = jnp.where(iota((128, slots), 1) % CAP == iota((128, slots), 0) % CAP, mine, 0.0)
    gather = ones_where(iota((8, 128), 1) // CAP == iota((8, 128), 0))
    out = mm(gather, mine.astype(BF16))
    return [out[k : k + 1] for k in range(6)]


def pair_of(hit0, value0, hit1, value1):
    return jnp.where(hit0, value0, jnp.where(hit1, value1, jnp.zeros((), value0.dtype)))


def gather_body(recv_ref, own_hbm, top_ref, bottom_ref, left_ref, right_ref, out_ref, own_ref, buffer, own_sem, out_sems, rim_ref, *matrices):
    slots = out_ref.shape[0]
    chunk = matrices[0].shape[0]
    load = pltpu.make_async_copy(own_hbm, own_ref, own_sem)
    load.start()
    rim_ref[0:64, :] = top_ref[...]
    rim_ref[64:128, :] = bottom_ref[...]
    rim_ref[128:192, :] = left_ref[...]
    rim_ref[192:256, :] = right_ref[...]
    tiles = recv_ref.shape[0] // 2
    cells = recv_ref[pl.ds(1, tiles, stride=2), :].astype(BF16)
    row, lane = iota((16, tiles), 0), iota((16, tiles), 1)
    for i, side in enumerate((-1, 1)):
        source = jnp.where(row == 0, diagonal(-1, side), jnp.where(row == 1, diagonal(1, side), -1))
        rim_ref[256 + 16 * i : 272 + 16 * i, :] = mm(ones_where(lane == source), cells).astype(BF16)
    rim_ref[288:384, :] = jnp.zeros((96, rim_ref.shape[1]), BF16)
    recv = recv_ref[pl.ds(0, tiles, stride=2), :].astype(BF16)
    lane = iota((chunk, 128), 1).astype(F32)
    upper = jnp.where(lane >= 64.0, 1.0, 0.0)
    in_row = (lane - 64.0 * upper).astype(BF16)
    upper = upper.astype(BF16)
    lane = lane.astype(BF16)

    def build(first, matrix_ref):
        w0, w1, w2, w3, row, col = [f.astype(BF16) for f in fields_by_row(recv, first, chunk)]
        at0, at1 = in_row == col - 1.0, in_row == col
        p0 = pair_of(at0, w0, at1, w2)
        p1 = pair_of(at0, w1, at1, w3)
        zero = jnp.zeros((), BF16)
        edge = 65.0 * upper
        matrix_ref[:, 4096:4224] = pair_of(edge == row, p0, edge == row + 1.0, p1)
        high = upper > 0.5
        side = pair_of(in_row == row - 1.0, jnp.where(high, w2, w0), in_row == row, jnp.where(high, w3, w1))
        matrix_ref[:, 4224:4352] = jnp.where(col == 64.0 * upper, side, zero)
        corner = pair_of(lane == 0.0, w0, lane == 1.0, w1) + pair_of(lane == 16.0, w2, lane == 17.0, w3)
        at_col = jnp.where(lane < 16.0, zero, zero + 64.0)
        odd = jnp.where(lane < 16.0, lane, lane - 16.0)
        matrix_ref[:, 4352:4480] = jnp.where(row == 64.0 * odd, jnp.where(col == at_col, corner, zero), zero)
        offset = row - upper
        for j in range(32):
            matrix_ref[:, 128 * j : 128 * j + 128] = pair_of(offset == 2.0 * j + 1.0, p0, offset == 2.0 * j, p1)

    def use(first, matrix_ref):
        out = mm(matrix_ref[:, :4096], own_ref[...]) + mm(matrix_ref[:, 4096:], rim_ref[...])
        at = slice(first, first + chunk)
        buffer[at, :] = out.astype(BF16)
        copies.append(pltpu.make_async_copy(buffer.at[at, :], out_ref.at[at, :], out_sems.at[len(copies)]))
        copies[-1].start()

    copies = []
    count = slots // chunk
    build(0, matrices[0])
    load.wait()
    for i in range(count):
        if i + 1 < count:
            build((i + 1) * chunk, matrices[i + 1])
        use(i * chunk, matrices[i])
    for copy in copies:
        copy.wait()


def components_body(spectra_ref, basis_ref, place_ref, pcs_ref, buffer, basis_buffer, sems, basis_sem):
    obs = spectra_ref.shape[0]
    blocks = buffer.shape[0]
    rows = obs // blocks

    def load(i):
        at = pl.ds(pl.multiple_of(i * rows, rows), rows)
        return pltpu.make_async_copy(spectra_ref.at[at, :], buffer.at[i], sems.at[i])

    basis = pltpu.make_async_copy(basis_ref, basis_buffer, basis_sem)
    basis.start()
    load(0).start()
    load(1).start()
    basis.wait()

    def step(i, carry):
        load(i).wait()

        @pl.when(i + 2 < blocks)
        def _():
            load(i + 2).start()

        at = pl.ds(pl.multiple_of(i * rows, rows), rows)
        pcs_ref[at, :] = mm(buffer[i], basis_buffer[...]).astype(BF16)
        return carry

    lax.fori_loop(0, blocks, step, 0)


def network_body(recv_ref, place_ref, pcs_ref, inv_ref, w_in_hbm, b_in_ref, w_out_hbm, b_out_ref, dep_ref, send_ref, pack_ref, unpack_ref, w_in_ref, w_out_ref, g_ref, dep_buffer, send_buffer, w_sems, dep_sems, send_sems):
    slots = recv_ref.shape[0]
    obs = pcs_ref.shape[0]
    loads = [pltpu.make_async_copy(w_in_hbm, w_in_ref, w_sems.at[0]), pltpu.make_async_copy(w_out_hbm, w_out_ref, w_sems.at[1])]
    for copy in loads:
        copy.start()
    inv = inv_ref[...]
    copies = []
    block = obs // 4
    place = place_ref[...]
    wide = jnp.broadcast_to(place.astype(F32), (128, obs)).T
    lane = iota((block, 128), 1).astype(F32)
    for i in range(4):
        at = slice(i * block, (i + 1) * block)
        for b in range(slots // 128):
            unpack_ref[at, 128 * b : 128 * b + 128] = ones_where(wide[at] - 128.0 * b == lane)
        half = slots // 4
        pack_ref[i * half : (i + 1) * half, :] = ones_where(iota((half, obs), 0) + i * half == place)
        column = mm(unpack_ref[at, :], recv_ref[...]).astype(BF16)
        if i == 0:
            for copy in loads:
                copy.wait()
        pre = mm(column, w_in_ref[...]) + b_in_ref[...]
        sig = jax.nn.sigmoid(pre)
        hidden = (pre * sig).astype(BF16)
        sim = mm(hidden, w_out_ref[...]) + b_out_ref[...]
        dep = (sim - pcs_ref[at, :].astype(F32)) * inv
        dep_buffer[at, :] = dep.astype(BF16)
        copies.append(pltpu.make_async_copy(dep_buffer.at[at, :], dep_ref.at[at, :], dep_sems.at[i]))
        copies[-1].start()
        g_sim = (dep * inv).astype(BF16)
        g_hidden = lax.dot_general(g_sim, w_out_ref[...], NT, preferred_element_type=F32)
        g_pre = (g_hidden * sig * (1.0 + pre * (1.0 - sig))).astype(BF16)
        g_ref[at, :] = lax.dot_general(g_pre, w_in_ref[...], NT, preferred_element_type=F32).astype(BF16)
    block = slots // 4
    for i in range(4):
        at = slice(i * block, (i + 1) * block)
        send_buffer[at, :] = mm(pack_ref[at, :], g_ref[...]).astype(BF16)
        copies.append(pltpu.make_async_copy(send_buffer.at[at, :], send_ref.at[at, :], send_sems.at[i]))
        copies[-1].start()
    for copy in copies:
        copy.wait()


def prepare_body(recv_ref, fields_ref):
    fields = fields_by_lane(recv_ref[pl.ds(0, recv_ref.shape[0] // 2, stride=2), :].astype(BF16), fields_ref.shape[1])
    fields_ref[...] = jnp.concatenate(fields + [fields[5], fields[5]], 0)


def scatter_rim_body(fields_ref, g_ref, up_ref, down_ref, left_ref, right_ref, rim_ref):
    slots = g_ref.shape[0]
    w0, w1, w2, w3, row, col = [fields_ref[k : k + 1, :].astype(BF16) for k in range(6)]
    zero = jnp.zeros((), BF16)
    sub = iota((64, slots), 0).astype(F32).astype(BF16)
    at0, at1 = sub == row - 1.0, sub == row
    rim_ref[128:192, :] = jnp.where(col == 0.0, pair_of(at0, w0, at1, w1), zero)
    rim_ref[208:272, :] = jnp.where(col == 64.0, pair_of(at0, w2, at1, w3), zero)
    low = iota((16, slots), 0).astype(F32).astype(BF16)
    first, last = jnp.where(row == 0.0, zero, zero - 1.0), jnp.where(row == 64.0, zero + 1.0, zero - 1.0)
    rim_ref[192:208, :] = jnp.where(col == 0.0, pair_of(low == first, w0, low == last, w1), zero)
    rim_ref[272:288, :] = jnp.where(col == 64.0, pair_of(low == first, w2, low == last, w3), zero)
    at0, at1 = sub == col - 1.0, sub == col
    rim_ref[0:64, :] = jnp.where(row == 0.0, pair_of(at0, w0, at1, w2), zero)
    rim_ref[64:128, :] = jnp.where(row == 64.0, pair_of(at0, w1, at1, w3), zero)
    out = mm(rim_ref[...], g_ref[...])
    up_ref[...] = out[0:64]
    down_ref[...] = out[64:128]
    left_ref[...] = out[128:208].astype(BF16)
    right_ref[...] = out[208:288].astype(BF16)


def corner_body(up_ref, down_ref, left_ref, right_ref, up_out, down_out):
    at = iota((64, 128), 0)
    left = left_ref[64:80, :].astype(F32)
    right = right_ref[64:80, :].astype(F32)
    for k, (ref, out) in enumerate(((up_ref, up_out), (down_ref, down_out))):
        extra = jnp.where(at == 0, left[k : k + 1], jnp.where(at == 63, right[k : k + 1], 0.0))
        out[...] = (ref[...] + extra).astype(BF16)


def scatter_body(half, fields_ref, g_ref, *refs):
    out_ref, buffer, sems = refs[-5:-2]
    matrices = refs[-2:]
    slots = g_ref.shape[0]
    rows = 16
    w0, w1, w2, w3, row, col = [fields_ref[k : k + 1, :].astype(BF16) for k in range(6)]
    sub = iota((64, slots), 0).astype(F32).astype(BF16)
    at0, at1 = sub == col - 1.0, sub == col
    p0 = pair_of(at0, w0, at1, w2)
    p1 = pair_of(at0, w1, at1, w3)
    row = jnp.broadcast_to(row, (64, slots))

    def build(first, matrix_ref):
        for j in range(rows):
            at = float(first + j)
            matrix_ref[64 * j : 64 * j + 64, :] = pair_of(row == at + 1.0, p0, row == at, p1)

    copies = []
    build(32 * half, matrices[0])
    for i in range(2):
        first = 32 * half + rows * i
        if i == 0:
            build(first + rows, matrices[1])
        out = mm(matrices[i][...], g_ref[...])
        buffer[i] = out.reshape(rows, 64, out.shape[1])
        copies.append(pltpu.make_async_copy(buffer.at[i], out_ref.at[pl.ds(first, rows)], sems.at[i]))
        copies[i].start()
    for copy in copies:
        copy.wait()


def edge_body(left_ref, right_ref, above_ref, below_ref, grad_ref, out_ref, sides, rows, in_sems, out_sems):
    edges = [
        (out_ref.at[:, pl.ds(0, 8), :], sides.at[0]),
        (out_ref.at[:, pl.ds(56, 8), :], sides.at[1]),
        (out_ref.at[0, pl.ds(8, 48), :], rows.at[0]),
        (out_ref.at[63, pl.ds(8, 48), :], rows.at[1]),
    ]
    loads = [pltpu.make_async_copy(a, b, in_sems.at[i]) for i, (a, b) in enumerate(edges)]
    stores = [pltpu.make_async_copy(b, a, out_sems.at[i]) for i, (a, b) in enumerate(edges)]
    for copy in loads:
        copy.start()
    for copy in loads:
        copy.wait()
    above, below = above_ref[...].astype(F32), below_ref[...].astype(F32)
    sides[0, :, 0, :] += left_ref[0:64, :].astype(F32)
    sides[1, :, 7, :] += right_ref[0:64, :].astype(F32)
    sides[0, 0] += above[0:8]
    sides[1, 0] += above[56:64]
    sides[0, 63] += below[0:8]
    sides[1, 63] += below[56:64]
    rows[0] += above[8:56]
    rows[1] += below[8:56]
    for copy in stores:
        copy.start()
    for copy in stores:
        copy.wait()


def in_hbm(x):
    return pltpu.with_memory_space_constraint(x, pltpu.HBM)


def shift(x, axis, step, closed):
    count = lax.axis_size(axis)
    pairs = [(i, (i + step) % count) for i in range(count) if closed or 0 <= i + step < count]
    return lax.ppermute(x, axis, pairs)


def exchange(x):
    return lax.all_to_all(x, AXES, split_axis=0, concat_axis=0, tiled=True)


def per_device(
    spectra,
    pc_basis,
    destination,
    corner_row,
    corner_col,
    corner_weight,
    state,
    inv_sigma,
    w_in,
    b_in,
    w_out,
    b_out,
):
    tiles = lax.axis_size("lat") * lax.axis_size("lon")
    obs = spectra.shape[0]
    npc = pc_basis.shape[1]
    levels = state.shape[2]
    slots = tiles * CAP
    sds = jax.ShapeDtypeStruct

    vmem = pl.BlockSpec(memory_space=pltpu.VMEM)
    hbm = pl.BlockSpec(memory_space=pltpu.HBM)
    send_meta, place, first, last, head, tail = call(
        route_body,
        (pltpu.HBM((2 * tiles, 128), F32), sds((1, obs), I32)) + (sds((64, levels), BF16),) * 4,
        destination.reshape(1, obs),
        corner_row.reshape(1, obs),
        corner_col.reshape(1, obs),
        corner_weight.T,
        in_hbm(state),
        specs=[vmem] * 4 + [hbm],
        scratch=[
            pltpu.VMEM((2, 64, 8, levels), BF16),
            pltpu.VMEM((2, 64, levels), BF16),
            pltpu.SemaphoreType.DMA((4,)),
        ],
        grant=None,
    )
    recv_meta = exchange(send_meta.reshape(tiles, 2, 128)).reshape(2 * tiles, 128)
    left = shift(last, "lon", 1, True)
    right = shift(first, "lon", -1, True)
    top = shift(tail, "lat", 1, False)
    bottom = shift(head, "lat", -1, False)

    columns = call(
        gather_body,
        pltpu.HBM((slots, levels), BF16),
        recv_meta,
        in_hbm(state.reshape(-1, levels)),
        top,
        bottom,
        left,
        right,
        specs=[vmem, hbm, vmem, vmem, vmem, vmem],
        outs=hbm,
        scratch=[
            pltpu.VMEM((4096, levels), BF16),
            pltpu.VMEM((slots, levels), BF16),
            pltpu.SemaphoreType.DMA,
            pltpu.SemaphoreType.DMA((4,)),
            pltpu.VMEM((384, levels), BF16),
        ]
        + [pltpu.VMEM((slots // 4, 4480), BF16)] * 4,
        grant=28,
    )
    columns, place = lax.optimization_barrier((columns, place))
    recv_columns = exchange(columns.reshape(tiles, CAP, levels)).reshape(slots, levels)
    pcs = call(
        components_body,
        sds((obs, npc), BF16),
        in_hbm(spectra),
        in_hbm(pc_basis),
        place,
        specs=[hbm, hbm, vmem],
        scratch=[
            pltpu.VMEM((4, obs // 4, spectra.shape[1]), BF16),
            pltpu.VMEM(pc_basis.shape, BF16),
            pltpu.SemaphoreType.DMA((4,)),
            pltpu.SemaphoreType.DMA,
        ],
        grant=26,
    )
    departures, send_g = call(
        network_body,
        (pltpu.HBM((obs, npc), BF16), pltpu.HBM((slots, levels), BF16)),
        recv_columns,
        place,
        pcs,
        inv_sigma[None],
        in_hbm(w_in),
        b_in[None],
        in_hbm(w_out),
        b_out[None],
        specs=[vmem] * 4 + [hbm, vmem, hbm, vmem],
        outs=(hbm, hbm),
        scratch=[
            pltpu.VMEM((slots, obs), BF16),
            pltpu.VMEM((obs, slots), BF16),
            pltpu.VMEM(w_in.shape, BF16),
            pltpu.VMEM(w_out.shape, BF16),
            pltpu.VMEM((obs, levels), BF16),
            pltpu.VMEM((obs, npc), BF16),
            pltpu.VMEM((slots, levels), BF16),
            pltpu.SemaphoreType.DMA((2,)),
            pltpu.SemaphoreType.DMA((4,)),
            pltpu.SemaphoreType.DMA((4,)),
        ],
        grant=24,
    )
    send_g, recv_meta = lax.optimization_barrier((send_g, recv_meta))
    g = exchange(send_g.reshape(tiles, CAP, levels)).reshape(slots, levels)
    fields = call(prepare_body, sds((8, slots), F32), recv_meta)
    up, down, g_left, g_right = call(
        scatter_rim_body,
        (sds((64, levels), F32), sds((64, levels), F32), sds((80, levels), BF16), sds((80, levels), BF16)),
        fields,
        g,
        scratch=[pltpu.VMEM((288, slots), BF16)],
    )
    from_right = shift(g_left, "lon", -1, True)
    from_left = shift(g_right, "lon", 1, True)
    half = [pltpu.VMEM((2, 16, 64, levels), F32), pltpu.SemaphoreType.DMA((2,))]
    half += [pltpu.VMEM((1024, slots), BF16)] * 2
    gradient = call(
        functools.partial(scatter_body, 0),
        pltpu.HBM((64, 64, levels), F32),
        fields,
        g,
        outs=hbm,
        scratch=half,
        grant=14,
    )
    from_left, from_right, gradient = lax.optimization_barrier((from_left, from_right, gradient))
    up, down = call(corner_body, (sds((64, levels), BF16), sds((64, levels), BF16)), up, down, from_left, from_right)
    up, down, g = lax.optimization_barrier((up, down, g))
    from_below = shift(up, "lat", -1, False)
    from_above = shift(down, "lat", 1, False)
    gradient = call(
        functools.partial(scatter_body, 1),
        pltpu.HBM((64, 64, levels), F32),
        fields,
        g,
        in_hbm(gradient),
        specs=[vmem, vmem, hbm],
        outs=hbm,
        scratch=half,
        grant=14,
        alias={2: 0},
    )
    gradient = call(
        edge_body,
        pltpu.HBM((64, 64, levels), F32),
        from_left,
        from_right,
        from_above,
        from_below,
        in_hbm(gradient),
        specs=[vmem, vmem, vmem, vmem, hbm],
        outs=hbm,
        scratch=[
            pltpu.VMEM((2, 64, 8, levels), F32),
            pltpu.VMEM((2, 48, levels), F32),
            pltpu.SemaphoreType.DMA((4,)),
            pltpu.SemaphoreType.DMA((4,)),
        ],
        alias={4: 0},
    )
    return (departures, gradient)


def solution(mesh):
    return jax.shard_map(
        per_device,
        mesh=mesh,
        in_specs=(
            P(AXES, None),
            P(),
            P(AXES, None),
            P(AXES),
            P(AXES),
            P(AXES, None),
            P("lat", "lon", None),
            P(),
            P(),
            P(),
            P(),
            P(),
        ),
        out_specs=(P(AXES, None), P("lat", "lon", None)),
        check_vma=False,
    )
```

```python
import functools

import jax
import jax.numpy as jnp
from jax import lax
from jax.experimental import pallas as pl
from jax.experimental.pallas import tpu as pltpu
from jax.sharding import PartitionSpec as P

CAP = 16
F32 = jnp.float32
BF16 = jnp.bfloat16
I32 = jnp.int32
NT = (((1,), (1,)), ((), ()))
AXES = ("lat", "lon")


def iota(shape, dim):
    return lax.broadcasted_iota(I32, shape, dim)


def mm(a, b):
    return jnp.dot(a, b, preferred_element_type=F32)


def ones_where(mask):
    return jnp.where(mask, 1.0, 0.0).astype(BF16)


def call(body, out_shape, *args, scratch=(), specs=None, outs=None, grant=8, alias=None):
    vmem = pl.BlockSpec(memory_space=pltpu.VMEM)
    return pl.pallas_call(
        body,
        in_specs=specs or [vmem] * len(args),
        out_specs=outs or jax.tree.map(lambda s: vmem, out_shape),
        out_shape=out_shape,
        scratch_shapes=scratch,
        input_output_aliases=alias or {},
        compiler_params=pltpu.CompilerParams(vmem_limit_bytes=grant << 20) if grant else None,
    )(*args)


def diagonal(rows, cols):
    lat, lon, n_lat, n_lon = lax.axis_index("lat"), lax.axis_index("lon"), lax.axis_size("lat"), lax.axis_size("lon")
    to = lat + rows
    return jnp.where((to >= 0) & (to < n_lat), to * n_lon + (lon + cols + n_lon) % n_lon, -1)


def route_body(dest_ref, row_ref, col_ref, weight_ref, state_ref, send_ref, place_ref, first_ref, last_ref, head_ref, tail_ref, sides, rows, sems):
    edges = [
        (state_ref.at[:, pl.ds(0, 8), :], sides.at[0]),
        (state_ref.at[:, pl.ds(56, 8), :], sides.at[1]),
        (state_ref.at[0], rows.at[0]),
        (state_ref.at[63], rows.at[1]),
    ]
    copies = [pltpu.make_async_copy(a, b, sems.at[i]) for i, (a, b) in enumerate(edges)]
    for copy in copies:
        copy.start()
    dest = dest_ref[...]
    tiles = send_ref.shape[0] // 2
    obs = dest.shape[1]
    onehot = jnp.where(iota((tiles, obs), 0) == dest, 1.0, 0.0)
    before = ones_where(iota((obs, obs), 0) < iota((obs, obs), 1))
    rank = mm(onehot.astype(BF16), before)
    slot = jnp.sum(onehot * rank, axis=0, keepdims=True).astype(I32)
    place_ref[...] = dest * CAP + slot
    here = iota((CAP, obs), 0) == slot
    weights = weight_ref[...].astype(F32)
    fields = [weights[k : k + 1] for k in range(4)]
    fields += [row_ref[...].astype(F32), col_ref[...].astype(F32)]
    parts = [jnp.where(here, field, 0.0) for field in fields]
    parts.append(jnp.zeros((128 - CAP * len(parts), obs), F32))
    table = jnp.concatenate(parts, 0).astype(BF16)
    send_ref[pl.ds(0, tiles, stride=2), :] = lax.dot_general(
        onehot.astype(BF16), table, NT, preferred_element_type=F32
    )
    for copy in copies:
        copy.wait()
    first_ref[...] = sides[0, :, 0, :]
    last_ref[...] = sides[1, :, 7, :]
    head_ref[...] = rows[0]
    tail_ref[...] = rows[1]
    row = iota((tiles, 128), 0)
    extra = jnp.zeros((tiles, 128), F32)
    for r in range(2):
        for c in range(2):
            cell = sides[c, 63 * r].astype(F32)[7 * c][None]
            extra = jnp.where(row == diagonal(2 * r - 1, 2 * c - 1), cell, extra)
    send_ref[pl.ds(1, tiles, stride=2), :] = extra


def fields_by_row(recv, first, count):
    tiles = recv.shape[0]
    pick = ones_where((iota((count, tiles), 0) + first) // CAP == iota((count, tiles), 1))
    mine = mm(pick, recv)
    mine = jnp.where(iota((count, 128), 0) % CAP == iota((count, 128), 1) % CAP, mine, 0.0)
    spread = ones_where(iota((128, 768), 0) // CAP == iota((128, 768), 1) // 128)
    out = mm(mine.astype(BF16), spread)
    return [out[:, 128 * k : 128 * k + 128] for k in range(6)]


def fields_by_lane(recv, slots):
    tiles = recv.shape[0]
    pick = ones_where(iota((tiles, slots), 1) // CAP == iota((tiles, slots), 0))
    mine = mm(recv.astype(F32).T.astype(BF16), pick)
    mine = jnp.where(iota((128, slots), 1) % CAP == iota((128, slots), 0) % CAP, mine, 0.0)
    gather = ones_where(iota((8, 128), 1) // CAP == iota((8, 128), 0))
    out = mm(gather, mine.astype(BF16))
    return [out[k : k + 1] for k in range(6)]


def pair_of(hit0, value0, hit1, value1):
    return jnp.where(hit0, value0, jnp.where(hit1, value1, jnp.zeros((), value0.dtype)))


def gather_body(recv_ref, own_hbm, top_ref, bottom_ref, left_ref, right_ref, out_ref, own_ref, buffer, own_sem, out_sems, rim_ref, *matrices):
    sizes = [m.shape[0] for m in matrices]
    firsts = [sum(sizes[:i]) for i in range(len(sizes))]
    load = pltpu.make_async_copy(own_hbm, own_ref, own_sem)
    load.start()
    rim_ref[0:64, :] = top_ref[...]
    rim_ref[64:128, :] = bottom_ref[...]
    rim_ref[128:192, :] = left_ref[...]
    rim_ref[192:256, :] = right_ref[...]
    tiles = recv_ref.shape[0] // 2
    cells = recv_ref[pl.ds(1, tiles, stride=2), :].astype(BF16)
    row, lane = iota((16, tiles), 0), iota((16, tiles), 1)
    for i, side in enumerate((-1, 1)):
        source = jnp.where(row == 0, diagonal(-1, side), jnp.where(row == 1, diagonal(1, side), -1))
        rim_ref[256 + 16 * i : 272 + 16 * i, :] = mm(ones_where(lane == source), cells).astype(BF16)
    rim_ref[288:384, :] = jnp.zeros((96, rim_ref.shape[1]), BF16)
    recv = recv_ref[pl.ds(0, tiles, stride=2), :].astype(BF16)
    lanes = iota((max(sizes), 128), 1).astype(F32)
    upper = jnp.where(lanes >= 64.0, 1.0, 0.0)
    in_rows = (lanes - 64.0 * upper).astype(BF16)
    uppers = upper.astype(BF16)
    lanes = lanes.astype(BF16)

    def build(first, matrix_ref):
        chunk = matrix_ref.shape[0]
        lane, in_row, upper = lanes[:chunk], in_rows[:chunk], uppers[:chunk]
        w0, w1, w2, w3, row, col = [f.astype(BF16) for f in fields_by_row(recv, first, chunk)]
        at0, at1 = in_row == col - 1.0, in_row == col
        p0 = pair_of(at0, w0, at1, w2)
        p1 = pair_of(at0, w1, at1, w3)
        zero = jnp.zeros((), BF16)
        edge = 65.0 * upper
        matrix_ref[:, 4096:4224] = pair_of(edge == row, p0, edge == row + 1.0, p1)
        high = upper > 0.5
        side = pair_of(in_row == row - 1.0, jnp.where(high, w2, w0), in_row == row, jnp.where(high, w3, w1))
        matrix_ref[:, 4224:4352] = jnp.where(col == 64.0 * upper, side, zero)
        corner = pair_of(lane == 0.0, w0, lane == 1.0, w1) + pair_of(lane == 16.0, w2, lane == 17.0, w3)
        at_col = jnp.where(lane < 16.0, zero, zero + 64.0)
        odd = jnp.where(lane < 16.0, lane, lane - 16.0)
        matrix_ref[:, 4352:4480] = jnp.where(row == 64.0 * odd, jnp.where(col == at_col, corner, zero), zero)
        offset = row - upper
        for j in range(32):
            matrix_ref[:, 128 * j : 128 * j + 128] = pair_of(offset == 2.0 * j + 1.0, p0, offset == 2.0 * j, p1)

    def use(first, matrix_ref):
        out = mm(matrix_ref[:, :4096], own_ref[...]) + mm(matrix_ref[:, 4096:], rim_ref[...])
        at = slice(first, first + matrix_ref.shape[0])
        buffer[at, :] = out.astype(BF16)
        copies.append(pltpu.make_async_copy(buffer.at[at, :], out_ref.at[at, :], out_sems.at[len(copies)]))
        copies[-1].start()

    copies = []
    count = len(sizes)
    build(0, matrices[0])
    load.wait()
    for i in range(count):
        if i + 1 < count:
            build(firsts[i + 1], matrices[i + 1])
        use(firsts[i], matrices[i])
    for copy in copies:
        copy.wait()


def components_body(spectra_ref, basis_ref, place_ref, pcs_ref, buffer, basis_buffer, sems, basis_sem):
    obs = spectra_ref.shape[0]
    blocks = buffer.shape[0]
    rows = obs // blocks

    def load(i):
        at = pl.ds(pl.multiple_of(i * rows, rows), rows)
        return pltpu.make_async_copy(spectra_ref.at[at, :], buffer.at[i], sems.at[i])

    basis = pltpu.make_async_copy(basis_ref, basis_buffer, basis_sem)
    basis.start()
    load(0).start()
    load(1).start()
    basis.wait()

    def step(i, carry):
        load(i).wait()

        @pl.when(i + 2 < blocks)
        def _():
            load(i + 2).start()

        at = pl.ds(pl.multiple_of(i * rows, rows), rows)
        pcs_ref[at, :] = mm(buffer[i], basis_buffer[...]).astype(BF16)
        return carry

    lax.fori_loop(0, blocks, step, 0)


def network_body(recv_ref, place_ref, pcs_ref, inv_ref, w_in_hbm, b_in_ref, w_out_hbm, b_out_ref, dep_ref, send_ref, pack_ref, unpack_ref, w_in_ref, w_out_ref, g_ref, dep_buffer, send_buffer, w_sems, dep_sems, send_sems):
    slots = recv_ref.shape[0]
    obs = pcs_ref.shape[0]
    loads = [pltpu.make_async_copy(w_in_hbm, w_in_ref, w_sems.at[0]), pltpu.make_async_copy(w_out_hbm, w_out_ref, w_sems.at[1])]
    for copy in loads:
        copy.start()
    inv = inv_ref[...]
    copies = []
    block = obs // 4
    place = place_ref[...]
    wide = jnp.broadcast_to(place.astype(F32), (128, obs)).T
    lane = iota((block, 128), 1).astype(F32)
    for i in range(4):
        at = slice(i * block, (i + 1) * block)
        for b in range(slots // 128):
            unpack_ref[at, 128 * b : 128 * b + 128] = ones_where(wide[at] - 128.0 * b == lane)
        half = slots // 4
        pack_ref[i * half : (i + 1) * half, :] = ones_where(iota((half, obs), 0) + i * half == place)
        column = mm(unpack_ref[at, :], recv_ref[...]).astype(BF16)
        if i == 0:
            for copy in loads:
                copy.wait()
        pre = mm(column, w_in_ref[...]) + b_in_ref[...]
        sig = jax.nn.sigmoid(pre)
        hidden = (pre * sig).astype(BF16)
        sim = mm(hidden, w_out_ref[...]) + b_out_ref[...]
        dep = (sim - pcs_ref[at, :].astype(F32)) * inv
        dep_buffer[at, :] = dep.astype(BF16)
        copies.append(pltpu.make_async_copy(dep_buffer.at[at, :], dep_ref.at[at, :], dep_sems.at[i]))
        copies[-1].start()
        g_sim = (dep * inv).astype(BF16)
        g_hidden = lax.dot_general(g_sim, w_out_ref[...], NT, preferred_element_type=F32)
        g_pre = (g_hidden * sig * (1.0 + pre * (1.0 - sig))).astype(BF16)
        g_ref[at, :] = lax.dot_general(g_pre, w_in_ref[...], NT, preferred_element_type=F32).astype(BF16)
    block = slots // 4
    for i in range(4):
        at = slice(i * block, (i + 1) * block)
        send_buffer[at, :] = mm(pack_ref[at, :], g_ref[...]).astype(BF16)
        copies.append(pltpu.make_async_copy(send_buffer.at[at, :], send_ref.at[at, :], send_sems.at[i]))
        copies[-1].start()
    for copy in copies:
        copy.wait()


def prepare_body(recv_ref, fields_ref):
    fields = fields_by_lane(recv_ref[pl.ds(0, recv_ref.shape[0] // 2, stride=2), :].astype(BF16), fields_ref.shape[1])
    fields_ref[...] = jnp.concatenate(fields + [fields[5], fields[5]], 0)


def scatter_rim_body(fields_ref, g_ref, up_ref, down_ref, left_ref, right_ref, rim_ref):
    slots = g_ref.shape[0]
    w0, w1, w2, w3, row, col = [fields_ref[k : k + 1, :].astype(BF16) for k in range(6)]
    zero = jnp.zeros((), BF16)
    sub = iota((64, slots), 0).astype(F32).astype(BF16)
    at0, at1 = sub == row - 1.0, sub == row
    rim_ref[128:192, :] = jnp.where(col == 0.0, pair_of(at0, w0, at1, w1), zero)
    rim_ref[208:272, :] = jnp.where(col == 64.0, pair_of(at0, w2, at1, w3), zero)
    low = iota((16, slots), 0).astype(F32).astype(BF16)
    first, last = jnp.where(row == 0.0, zero, zero - 1.0), jnp.where(row == 64.0, zero + 1.0, zero - 1.0)
    rim_ref[192:208, :] = jnp.where(col == 0.0, pair_of(low == first, w0, low == last, w1), zero)
    rim_ref[272:288, :] = jnp.where(col == 64.0, pair_of(low == first, w2, low == last, w3), zero)
    at0, at1 = sub == col - 1.0, sub == col
    rim_ref[0:64, :] = jnp.where(row == 0.0, pair_of(at0, w0, at1, w2), zero)
    rim_ref[64:128, :] = jnp.where(row == 64.0, pair_of(at0, w1, at1, w3), zero)
    out = mm(rim_ref[...], g_ref[...])
    up_ref[...] = out[0:64]
    down_ref[...] = out[64:128]
    left_ref[...] = out[128:208].astype(BF16)
    right_ref[...] = out[208:288].astype(BF16)


def corner_body(up_ref, down_ref, left_ref, right_ref, up_out, down_out):
    at = iota((64, 128), 0)
    left = left_ref[64:80, :].astype(F32)
    right = right_ref[64:80, :].astype(F32)
    for k, (ref, out) in enumerate(((up_ref, up_out), (down_ref, down_out))):
        extra = jnp.where(at == 0, left[k : k + 1], jnp.where(at == 63, right[k : k + 1], 0.0))
        out[...] = (ref[...] + extra).astype(BF16)


def scatter_body(half, fields_ref, g_ref, *refs):
    out_ref, buffer, sems = refs[-5:-2]
    matrices = refs[-2:]
    slots = g_ref.shape[0]
    rows = 16
    w0, w1, w2, w3, row, col = [fields_ref[k : k + 1, :].astype(BF16) for k in range(6)]
    sub = iota((64, slots), 0).astype(F32).astype(BF16)
    at0, at1 = sub == col - 1.0, sub == col
    p0 = pair_of(at0, w0, at1, w2)
    p1 = pair_of(at0, w1, at1, w3)
    row = jnp.broadcast_to(row, (64, slots))

    def build(first, matrix_ref):
        for j in range(rows):
            at = float(first + j)
            matrix_ref[64 * j : 64 * j + 64, :] = pair_of(row == at + 1.0, p0, row == at, p1)

    copies = []
    build(32 * half, matrices[0])
    for i in range(2):
        first = 32 * half + rows * i
        if i == 0:
            build(first + rows, matrices[1])
        out = mm(matrices[i][...], g_ref[...])
        buffer[i] = out.reshape(rows, 64, out.shape[1])
        copies.append(pltpu.make_async_copy(buffer.at[i], out_ref.at[pl.ds(first, rows)], sems.at[i]))
        copies[i].start()
    for copy in copies:
        copy.wait()


def edge_body(left_ref, right_ref, above_ref, below_ref, grad_ref, out_ref, sides, rows, in_sems, out_sems):
    edges = [
        (out_ref.at[:, pl.ds(0, 8), :], sides.at[0]),
        (out_ref.at[:, pl.ds(56, 8), :], sides.at[1]),
        (out_ref.at[0, pl.ds(8, 48), :], rows.at[0]),
        (out_ref.at[63, pl.ds(8, 48), :], rows.at[1]),
    ]
    loads = [pltpu.make_async_copy(a, b, in_sems.at[i]) for i, (a, b) in enumerate(edges)]
    stores = [pltpu.make_async_copy(b, a, out_sems.at[i]) for i, (a, b) in enumerate(edges)]
    for copy in loads:
        copy.start()
    for copy in loads:
        copy.wait()
    above, below = above_ref[...].astype(F32), below_ref[...].astype(F32)
    sides[0, :, 0, :] += left_ref[0:64, :].astype(F32)
    sides[1, :, 7, :] += right_ref[0:64, :].astype(F32)
    sides[0, 0] += above[0:8]
    sides[1, 0] += above[56:64]
    sides[0, 63] += below[0:8]
    sides[1, 63] += below[56:64]
    rows[0] += above[8:56]
    rows[1] += below[8:56]
    for copy in stores:
        copy.start()
    for copy in stores:
        copy.wait()


def in_hbm(x):
    return pltpu.with_memory_space_constraint(x, pltpu.HBM)


def shift(x, axis, step, closed):
    count = lax.axis_size(axis)
    pairs = [(i, (i + step) % count) for i in range(count) if closed or 0 <= i + step < count]
    return lax.ppermute(x, axis, pairs)


def exchange(x):
    return lax.all_to_all(x, AXES, split_axis=0, concat_axis=0, tiled=True)


def per_device(
    spectra,
    pc_basis,
    destination,
    corner_row,
    corner_col,
    corner_weight,
    state,
    inv_sigma,
    w_in,
    b_in,
    w_out,
    b_out,
):
    tiles = lax.axis_size("lat") * lax.axis_size("lon")
    obs = spectra.shape[0]
    npc = pc_basis.shape[1]
    levels = state.shape[2]
    slots = tiles * CAP
    sds = jax.ShapeDtypeStruct

    vmem = pl.BlockSpec(memory_space=pltpu.VMEM)
    hbm = pl.BlockSpec(memory_space=pltpu.HBM)
    send_meta, place, first, last, head, tail = call(
        route_body,
        (pltpu.HBM((2 * tiles, 128), F32), sds((1, obs), I32)) + (sds((64, levels), BF16),) * 4,
        destination.reshape(1, obs),
        corner_row.reshape(1, obs),
        corner_col.reshape(1, obs),
        corner_weight.T,
        in_hbm(state),
        specs=[vmem] * 4 + [hbm],
        scratch=[
            pltpu.VMEM((2, 64, 8, levels), BF16),
            pltpu.VMEM((2, 64, levels), BF16),
            pltpu.SemaphoreType.DMA((4,)),
        ],
        grant=None,
    )
    recv_meta = exchange(send_meta.reshape(tiles, 2, 128)).reshape(2 * tiles, 128)
    left = shift(last, "lon", 1, True)
    right = shift(first, "lon", -1, True)
    top = shift(tail, "lat", 1, False)
    bottom = shift(head, "lat", -1, False)

    columns = call(
        gather_body,
        pltpu.HBM((slots, levels), BF16),
        recv_meta,
        in_hbm(state.reshape(-1, levels)),
        top,
        bottom,
        left,
        right,
        specs=[vmem, hbm, vmem, vmem, vmem, vmem],
        outs=hbm,
        scratch=[
            pltpu.VMEM((4096, levels), BF16),
            pltpu.VMEM((slots, levels), BF16),
            pltpu.SemaphoreType.DMA,
            pltpu.SemaphoreType.DMA((5,)),
            pltpu.VMEM((384, levels), BF16),
        ]
        + [pltpu.VMEM((slots // n, 4480), BF16) for n in (8, 4, 4, 4, 8)],
        grant=28,
    )
    columns, place = lax.optimization_barrier((columns, place))
    recv_columns = exchange(columns.reshape(tiles, CAP, levels)).reshape(slots, levels)
    pcs = call(
        components_body,
        sds((obs, npc), BF16),
        in_hbm(spectra),
        in_hbm(pc_basis),
        place,
        specs=[hbm, hbm, vmem],
        scratch=[
            pltpu.VMEM((4, obs // 4, spectra.shape[1]), BF16),
            pltpu.VMEM(pc_basis.shape, BF16),
            pltpu.SemaphoreType.DMA((4,)),
            pltpu.SemaphoreType.DMA,
        ],
        grant=26,
    )
    departures, send_g = call(
        network_body,
        (pltpu.HBM((obs, npc), BF16), pltpu.HBM((slots, levels), BF16)),
        recv_columns,
        place,
        pcs,
        inv_sigma[None],
        in_hbm(w_in),
        b_in[None],
        in_hbm(w_out),
        b_out[None],
        specs=[vmem] * 4 + [hbm, vmem, hbm, vmem],
        outs=(hbm, hbm),
        scratch=[
            pltpu.VMEM((slots, obs), BF16),
            pltpu.VMEM((obs, slots), BF16),
            pltpu.VMEM(w_in.shape, BF16),
            pltpu.VMEM(w_out.shape, BF16),
            pltpu.VMEM((obs, levels), BF16),
            pltpu.VMEM((obs, npc), BF16),
            pltpu.VMEM((slots, levels), BF16),
            pltpu.SemaphoreType.DMA((2,)),
            pltpu.SemaphoreType.DMA((4,)),
            pltpu.SemaphoreType.DMA((4,)),
        ],
        grant=24,
    )
    send_g, recv_meta = lax.optimization_barrier((send_g, recv_meta))
    g = exchange(send_g.reshape(tiles, CAP, levels)).reshape(slots, levels)
    fields = call(prepare_body, sds((8, slots), F32), recv_meta)
    up, down, g_left, g_right = call(
        scatter_rim_body,
        (sds((64, levels), F32), sds((64, levels), F32), sds((80, levels), BF16), sds((80, levels), BF16)),
        fields,
        g,
        scratch=[pltpu.VMEM((288, slots), BF16)],
    )
    from_right = shift(g_left, "lon", -1, True)
    from_left = shift(g_right, "lon", 1, True)
    half = [pltpu.VMEM((2, 16, 64, levels), F32), pltpu.SemaphoreType.DMA((2,))]
    half += [pltpu.VMEM((1024, slots), BF16)] * 2
    gradient = call(
        functools.partial(scatter_body, 0),
        pltpu.HBM((64, 64, levels), F32),
        fields,
        g,
        outs=hbm,
        scratch=half,
        grant=14,
    )
    from_left, from_right, gradient = lax.optimization_barrier((from_left, from_right, gradient))
    up, down = call(corner_body, (sds((64, levels), BF16), sds((64, levels), BF16)), up, down, from_left, from_right)
    up, down, g = lax.optimization_barrier((up, down, g))
    from_below = shift(up, "lat", -1, False)
    from_above = shift(down, "lat", 1, False)
    gradient = call(
        functools.partial(scatter_body, 1),
        pltpu.HBM((64, 64, levels), F32),
        fields,
        g,
        in_hbm(gradient),
        specs=[vmem, vmem, hbm],
        outs=hbm,
        scratch=half,
        grant=14,
        alias={2: 0},
    )
    gradient = call(
        edge_body,
        pltpu.HBM((64, 64, levels), F32),
        from_left,
        from_right,
        from_above,
        from_below,
        in_hbm(gradient),
        specs=[vmem, vmem, vmem, vmem, hbm],
        outs=hbm,
        scratch=[
            pltpu.VMEM((2, 64, 8, levels), F32),
            pltpu.VMEM((2, 48, levels), F32),
            pltpu.SemaphoreType.DMA((4,)),
            pltpu.SemaphoreType.DMA((4,)),
        ],
        alias={4: 0},
    )
    return (departures, gradient)


def solution(mesh):
    return jax.shard_map(
        per_device,
        mesh=mesh,
        in_specs=(
            P(AXES, None),
            P(),
            P(AXES, None),
            P(AXES),
            P(AXES),
            P(AXES, None),
            P("lat", "lon", None),
            P(),
            P(),
            P(),
            P(),
            P(),
        ),
        out_specs=(P(AXES, None), P("lat", "lon", None)),
        check_vma=False,
    )
```
